32 devices in a mesh: ta: 8 (over y, x, core), site: 4 (over z).
Axes of the slice: x: 2, y: 2, z: 4, core: 2. Of those that a mesh axis runs over, the one named last changes fastest.
Arguments:
- eigenvectors: bfloat16 [16, 192, 3, 4, 256], P('ta', None, None, 'site'), parts along dimension 0, may hold values from -6 to 6
- gauge_links: bfloat16 [16, 3, 3, 3, 4, 256], P('ta', None, None, None, 'site'), parts along dimension 0, may hold values from -2.5 to 2.5
- displacements: int32 [2, 3], replicated, may hold values from 0 to 3, as said below
- block_rows: int32 [4], replicated, may hold values from 0 to 191
Outputs:
- elementals: float32 [16, 4, 192, 384], P('ta', None, 'site'), parts along dimension 0
The draws below stay inside these ranges and needn't reach their ends.
There are 8 independent parts, one for each index of `ta`. The reference program is written for one: setup_inputs(seed, part) draws one part's arguments, and reference() takes and returns one part's arrays. A program takes and returns all parts, laid end to end along the dimension named above; an argument that names none is the same for every part. Nothing has to cross between parts.
Inputs may be any that keep to these rules, and one draw needn't show every extreme that they name: `displacements`: each combination displaces at least one of its three vectors along the third dimension.
All inputs are finite; a program needn't handle non-finite values.
Results may differ from the reference program's by a relative error of at most 0.012.
Values may be sent and summed in bfloat16 or wider, within the bound.
No kernel may reach another device: no remote copies, remote signals or barrier semaphores. Data moves between devices by JAX's collectives and lax.ppermute only.
A program may use at most 64 MiB of HBM per device.

```python
import math
import jax
import jax.numpy as jnp
from jax import lax

NV = 192
IB = 4
NCOMB = 2
LX = 16
LZ = 4
LXY = 256
VOL = 1024


def draw_displacements(key, part):
    directions = jax.random.randint(key, (NCOMB, 3), 0, 4)
    chosen_slot = jax.random.randint(jax.random.fold_in(key, 7), (NCOMB,), 0, 3)
    forced = jnp.arange(3)[None, :] == chosen_slot[:, None]
    return jnp.where(forced, 3, directions).astype(jnp.int32)


def touch_ends(values, rng, low, high):
    shape = values.shape
    spot = [jax.random.randint(jax.random.fold_in(rng, axis), (), 0, shape[axis]) for axis in range(len(shape))]
    values = values.at[tuple(spot)].set(low)
    longest = shape.index(max(shape))
    spot[longest] = (spot[longest] + 1) % shape[longest]
    return values.at[tuple(spot)].set(high)


def block_scale(rng, extent, split, smallest, high):
    gain = 1.0
    for position, parts in split:
        heights = jax.random.uniform(jax.random.fold_in(jax.random.fold_in(rng, 6), position), (parts,), jnp.float32, smallest / len(split), high / len(split))
        gain = gain * jnp.repeat(jnp.exp(heights), extent[position] // parts).reshape((-1,) + (1,) * (len(extent) - 1 - position))
    return gain


def gaussian(rng, extent, deviation, reach, pieces=(), kind=jnp.bfloat16):
    values = jax.random.normal(rng, extent, jnp.float32) * deviation
    if len(pieces) > 0:
        values = block_scale(rng, extent, pieces, -0.22, 0.18) * values
    return jnp.clip(values, min=-reach, max=reach).astype(kind)


def setup_inputs(seed: int = 0, part: int = 0) -> dict:
    streams_of = jax.random.split(jax.random.key(seed), 5)
    part_splits = jax.random.split(jax.random.fold_in(streams_of[4], part), 5)
    eigenvectors = gaussian(part_splits[0], (2, NV, 3, LZ, LXY), 1.0, 6.0, ((3, 4),))
    gauge_links = gaussian(part_splits[1], (2, 3, 3, 3, LZ, LXY), 6 ** -0.5, 2.5, ((4, 4),))
    displacements = draw_displacements(jax.random.fold_in(streams_of[4], 71), part)
    block_rows = touch_ends(jax.random.randint(streams_of[3], (IB,), 0, NV), jax.random.fold_in(streams_of[3], 1), 0, NV - 1).astype(jnp.int32)
    return {"eigenvectors": eigenvectors, "gauge_links": gauge_links, "displacements": displacements, "block_rows": block_rows}


def neighbours(vectors, direction, width_x):

    def along_x(values):
        shaped = values.reshape(values.shape[:-1] + (-1, width_x))
        return jnp.roll(shaped, -1, axis=-1).reshape(values.shape)

    def along_y(values):
        shaped = values.reshape(values.shape[:-1] + (-1, width_x))
        return jnp.roll(shaped, -1, axis=-2).reshape(values.shape)

    def along_z(values):
        return jnp.roll(values, -1, axis=3)
    return lax.switch(direction, [lambda values: values, along_x, along_y, along_z], vectors)

def displace(vectors, links, direction, width_x):
    moved = neighbours(vectors, direction, width_x).astype(jnp.float32)
    chosen = lax.dynamic_index_in_dim(links, jnp.maximum(direction - 1, 0), axis=1, keepdims=False).astype(jnp.float32)
    identity = jnp.eye(3, dtype=jnp.float32)[:, :, None, None]
    resting = direction == 0
    link_re = jnp.where(resting, identity, chosen[0])
    link_im = jnp.where(resting, jnp.zeros_like(chosen[1]), chosen[1])

    def multiply(matrix, component):
        return jnp.einsum('abzs,nbzs->nazs', matrix, component)
    out_re = multiply(link_re, moved[0]) - multiply(link_im, moved[1])
    out_im = multiply(link_re, moved[1]) + multiply(link_im, moved[0])
    return jnp.stack([out_re, out_im]).astype(jnp.bfloat16)

def cross_triple(left_field, mid_field):
    left_re = left_field[0].astype(jnp.float32)[:, None]
    left_im = left_field[1].astype(jnp.float32)[:, None]
    mid_re = mid_field[0].astype(jnp.float32)[None]
    mid_im = mid_field[1].astype(jnp.float32)[None]

    def product_re(first_color, second_color):
        return left_re[:, :, first_color] * mid_re[:, :, second_color] - left_im[:, :, first_color] * mid_im[:, :, second_color]

    def product_im(first_color, second_color):
        return left_re[:, :, first_color] * mid_im[:, :, second_color] + left_im[:, :, first_color] * mid_re[:, :, second_color]
    orders = ((1, 2), (2, 0), (0, 1))
    cross_re = jnp.stack([product_re(one, two) - product_re(two, one) for one, two in orders], axis=2)
    cross_im = jnp.stack([product_im(one, two) - product_im(two, one) for one, two in orders], axis=2)
    return jnp.stack([cross_re, cross_im], axis=2).astype(jnp.bfloat16)

def contract_sites(crossed, right_field):
    rows_count = crossed.shape[0] * crossed.shape[1]
    left = crossed.reshape(rows_count, -1)
    count_k = right_field.shape[1]
    right_re = right_field[0].reshape(count_k, -1)
    right_im = right_field[1].reshape(count_k, -1)
    upper = jnp.concatenate([right_re, -right_im], axis=1)
    lower = jnp.concatenate([right_im, right_re], axis=1)
    right = jnp.concatenate([upper, lower], axis=0)
    result = lax.dot_general(left, right, (((1,), (1,)), ((), ())), preferred_element_type=jnp.float32)
    return result.reshape(crossed.shape[0], crossed.shape[1], 2 * count_k)

def reference(eigenvectors, gauge_links, displacements, block_rows):
    picked = jnp.take(eigenvectors, block_rows, axis=1)
    results = []
    for combo in range(NCOMB):
        left_field = displace(picked, gauge_links, displacements[combo, 0], LX)
        mid_field = displace(eigenvectors, gauge_links, displacements[combo, 1], LX)
        right_field = displace(eigenvectors, gauge_links, displacements[combo, 2], LX)
        results.append(contract_sites(cross_triple(left_field, mid_field), right_field))
    scale = 1.0 / math.sqrt(24.0 * VOL)
    return jnp.stack(results) * scale
```

```python
import functools
import math

import jax
import jax.numpy as jnp
from jax import lax
from jax.experimental import pallas as pl
from jax.experimental.pallas import tpu as pltpu
from jax.sharding import PartitionSpec as P

LX = 16
COLORS = 3
TILE = 16
LANES = 128
SUBLANES = 8


def shifted(block, axis, distance):
    count = lax.axis_size(axis)
    return lax.ppermute(block, axis, [(i, (i + distance) % count) for i in range(count)])


def shift_matrix(direction, sites, width_x):
    source = lax.broadcasted_iota(jnp.int32, (sites, sites), 0)
    target = lax.broadcasted_iota(jnp.int32, (sites, sites), 1)
    column = lax.rem(target, width_x)
    along_x = target - column + lax.rem(column + 1, width_x)
    along_y = lax.rem(target + width_x, sites)
    neighbour = jnp.where(direction == 1, along_x, jnp.where(direction == 2, along_y, target))
    return jnp.where(source == neighbour, 1.0, 0.0).astype(jnp.bfloat16)


def mul(left, right):
    return left[0] * right[0] - left[1] * right[1], left[0] * right[1] + left[1] * right[0]


def add(left, right):
    return left[0] + right[0], left[1] + right[1]


def plane_of(here_ref, next_ref, direction, index):
    return jnp.where(direction == 3, next_ref[index], here_ref[index])


def chosen_link(links_ref, direction):
    which = jnp.maximum(direction - 1, 0)
    resting = direction == 0

    def entry(row, column):
        at = 2 * (COLORS * row + column)
        re = links_ref[which, at : at + 1, :]
        im = links_ref[which, at + 1 : at + 2, :]
        unit = jnp.full_like(re, 1.0 if row == column else 0.0)
        return jnp.where(resting, unit, re), jnp.where(resting, jnp.zeros_like(im), im)

    return [[entry(row, column) for column in range(COLORS)] for row in range(COLORS)]


def site_matrices(combo, moves, rows, here_ref, next_ref, links_ref, matrices_ref, scale, width_x):
    vectors, sites = here_ref.shape[-2:]
    direction = moves[combo, 0]
    picks = matrices_ref.shape[2]
    numbers = lax.broadcasted_iota(jnp.int32, (picks, vectors), 1)
    lane = lax.broadcasted_iota(jnp.int32, (picks, vectors), 0)
    wanted = jnp.full((picks, vectors), -1, jnp.int32)
    for i in range(rows.shape[0]):
        wanted = jnp.where(lane == i, rows[i], wanted)
    select = jnp.where(numbers == wanted, 1.0, 0.0).astype(jnp.bfloat16)
    shift = shift_matrix(direction, sites, width_x)

    def moved(part, color):
        picked = jnp.dot(
            select,
            plane_of(here_ref, next_ref, direction, (part, color)),
            preferred_element_type=jnp.float32,
        ).astype(jnp.bfloat16)
        return jnp.dot(picked, shift, preferred_element_type=jnp.float32)

    fields = [(moved(0, color), moved(1, color)) for color in range(COLORS)]
    first, second, third = (chosen_link(links_ref, moves[combo, slot]) for slot in range(3))

    def total(terms):
        return functools.reduce(add, terms)

    left = [
        total(mul(first[a][b], fields[b]) for b in range(COLORS)) for a in range(COLORS)
    ]
    for column in range(COLORS):
        after = []
        for b in range(COLORS):
            up, down = (b + 1) % COLORS, (b + 2) % COLORS
            plus = mul(third[up][column], left[down])
            minus = mul(third[down][column], left[up])
            after.append((plus[0] - minus[0], plus[1] - minus[1]))
        for row in range(COLORS):
            re, im = total(mul(second[b][row], after[b]) for b in range(COLORS))
            at = 2 * (COLORS * column + row)
            matrices_ref[combo, at] = re * scale
            matrices_ref[combo, at + 1] = im * scale


def right_operand(combo, moves, here_ref, next_ref, right_ref, width_x):
    vectors, sites = here_ref.shape[-2:]
    direction = moves[combo, 2]
    shift = shift_matrix(direction, sites, width_x)
    half = COLORS * sites
    for color in range(COLORS):
        at = color * sites
        re, im = (
            jnp.dot(
                plane_of(here_ref, next_ref, direction, (part, color)),
                shift,
                preferred_element_type=jnp.float32,
            )
            for part in range(2)
        )
        kind = right_ref.dtype
        right_ref[combo, :vectors, at : at + sites] = re.astype(kind)
        right_ref[combo, vectors:, half + at : half + at + sites] = re.astype(kind)
        right_ref[combo, :vectors, half + at : half + at + sites] = (-im).astype(kind)
        right_ref[combo, vectors:, at : at + sites] = im.astype(kind)


def row_block(combo, start, moves, here_ref, next_ref, matrices_ref, right_ref, mid_ref, crossed_ref, out_ref, width_x):
    sites = here_ref.shape[-1]
    picks, count = out_ref.shape[1:3]
    direction = moves[combo, 1]
    shift = shift_matrix(direction, sites, width_x)
    rows = pl.ds(pl.multiple_of(start, TILE), count)
    block = plane_of(here_ref, next_ref, direction, (slice(None), slice(None), rows))
    mid_ref[...] = jnp.dot(
        block.reshape(2 * COLORS * count, sites), shift, preferred_element_type=jnp.float32
    )
    for lanes in range(sites // LANES):
        across = slice(lanes * LANES, (lanes + 1) * LANES)
        for pick in range(picks):
            entries = [
                jnp.broadcast_to(matrices_ref[combo, at, pick : pick + 1, across], (TILE, LANES))
                for at in range(2 * COLORS * COLORS)
            ]
            for tile in range(count // TILE):
                field = [
                    tuple(
                        mid_ref[pl.ds((part * COLORS + color) * count + tile * TILE, TILE), across]
                        for part in range(2)
                    )
                    for color in range(COLORS)
                ]
                for column in range(COLORS):
                    re, im = functools.reduce(
                        add,
                        (
                            mul(
                                (
                                    entries[2 * (COLORS * column + row)],
                                    entries[2 * (COLORS * column + row) + 1],
                                ),
                                field[row],
                            )
                            for row in range(COLORS)
                        ),
                    )
                    down = slice(pick * count + tile * TILE, pick * count + (tile + 1) * TILE)
                    at = column * sites + lanes * LANES
                    crossed_ref[down, at : at + LANES] = re.astype(jnp.bfloat16)
                    at += COLORS * sites
                    crossed_ref[down, at : at + LANES] = im.astype(jnp.bfloat16)
    result = lax.dot_general(
        crossed_ref[...],
        right_ref[combo],
        (((1,), (1,)), ((), ())),
        preferred_element_type=jnp.float32,
    )
    out_ref[combo] = result.reshape(out_ref.shape[1:]).astype(out_ref.dtype)


def first_kernel(scale, width_x, starts, moves, rows, here_ref, next_ref, links_ref, right_ref, matrices_ref, out_ref, mid_ref, crossed_ref):
    def step(combo, carry):
        site_matrices(combo, moves, rows, here_ref, next_ref, links_ref, matrices_ref, scale, width_x)
        right_operand(combo, moves, here_ref, next_ref, right_ref, width_x)
        row_block(combo, starts[0], moves, here_ref, next_ref, matrices_ref, right_ref, mid_ref, crossed_ref, out_ref, width_x)
        return carry

    lax.fori_loop(0, out_ref.shape[0], step, 0)


def later_kernel(width_x, starts, moves, here_ref, next_ref, right_ref, matrices_ref, *rest):
    *outs, mid_ref, crossed_ref = rest

    def step(combo, carry):
        for number, out_ref in enumerate(outs):
            row_block(combo, starts[number], moves, here_ref, next_ref, matrices_ref, right_ref, mid_ref, crossed_ref, out_ref, width_x)
        return carry

    lax.fori_loop(0, outs[0].shape[0], step, 0)


def on_device(eigenvectors, gauge_links, displacements, block_rows):
    parts, vectors, colors, planes, sites = eigenvectors.shape
    ring = lax.axis_size("site")
    me = lax.axis_index("site")
    combos, picks = displacements.shape[0], block_rows.shape[0]
    count = vectors // ring
    sites_all = planes * ring * sites
    scale = 1.0 / math.sqrt(24.0 * sites_all)
    here = jnp.transpose(eigenvectors, (0, 2, 3, 1, 4)).reshape(parts, colors, vectors, sites)
    after = shifted(here, "site", -1)
    links = jnp.transpose(gauge_links, (1, 2, 3, 0, 4, 5)).astype(jnp.float32)
    links = links.reshape(COLORS, colors * colors * parts, sites)

    def chunk(kind):
        return jax.ShapeDtypeStruct((combos, picks, count, 2 * vectors), kind)

    def starts(offsets):
        return jnp.stack([lax.rem(me + offset, ring) * count for offset in offsets]).astype(jnp.int32)

    smem = pl.BlockSpec(memory_space=pltpu.SMEM)
    vmem = pl.BlockSpec(memory_space=pltpu.VMEM)
    scratch = [
        pltpu.VMEM((parts * colors * count, sites), jnp.float32),
        pltpu.VMEM((picks * count, parts * colors * sites), jnp.bfloat16),
    ]
    offsets = [ring // 2] + [o for o in range(1, ring) if o != ring // 2]
    right, matrices, sent = pl.pallas_call(
        functools.partial(first_kernel, scale, LX),
        out_shape=(
            jax.ShapeDtypeStruct((combos, 2 * vectors, parts * colors * sites), jnp.bfloat16),
            jax.ShapeDtypeStruct((combos, 2 * colors * colors, SUBLANES, sites), jnp.float32),
            chunk(jnp.bfloat16),
        ),
        in_specs=[smem, smem, smem, vmem, vmem, vmem],
        out_specs=(vmem, vmem, vmem),
        scratch_shapes=scratch,
        name="first",
    )(starts(offsets[:1]), displacements, block_rows, here, after, links)
    arrived = [shifted(sent, "site", offsets[0])]
    later = pl.pallas_call(
        functools.partial(later_kernel, LX),
        out_shape=tuple(chunk(jnp.bfloat16) for _ in offsets[1:]) + (chunk(jnp.float32),),
        in_specs=[smem, smem, vmem, vmem, vmem, vmem],
        out_specs=(vmem,) * len(offsets),
        scratch_shapes=scratch,
        cost_estimate=pl.CostEstimate(flops=4_000_000_000, bytes_accessed=8_000_000, transcendentals=0),
        name="later",
    )(starts(offsets[1:] + [0]), displacements, here, after, right, matrices)
    arrived += [shifted(block, "site", offset) for block, offset in zip(later[:-1], offsets[1:])]
    return functools.reduce(lambda total, block: total + block.astype(jnp.float32), arrived, later[-1])


def solution(mesh):
    return jax.shard_map(
        on_device,
        mesh=mesh,
        in_specs=(
            P("ta", None, None, "site", None),
            P("ta", None, None, None, "site", None),
            P(),
            P(),
        ),
        out_specs=P("ta", None, "site", None),
        check_vma=False,
    )
```

```python
import functools
import math

import jax
import jax.numpy as jnp
from jax import lax
from jax.experimental import pallas as pl
from jax.experimental.pallas import tpu as pltpu
from jax.sharding import PartitionSpec as P


LX = 16
COLORS = 3
TILE = 16
LANES = 128
SUBLANES = 8
VMEM_BYTES = 24 * 2**20


def shifted(block, axis, distance):
    count = lax.axis_size(axis)
    return lax.ppermute(block, axis, [(i, (i + distance) % count) for i in range(count)])


def shift_matrices(sites, width_x):
    source = lax.broadcasted_iota(jnp.int32, (COLORS, sites, sites), 1)
    target = lax.broadcasted_iota(jnp.int32, (COLORS, sites, sites), 2)
    direction = lax.broadcasted_iota(jnp.int32, (COLORS, sites, sites), 0)
    column = lax.rem(target, width_x)
    along_x = target - column + lax.rem(column + 1, width_x)
    along_y = lax.rem(target + width_x, sites)
    neighbour = jnp.where(direction == 1, along_x, jnp.where(direction == 2, along_y, target))
    return jnp.where(source == neighbour, 1.0, 0.0).astype(jnp.bfloat16)


def in_plane(shifts_ref, direction):
    return shifts_ref[jnp.where(direction == 3, 0, direction)]


def mul(left, right):
    return left[0] * right[0] - left[1] * right[1], left[0] * right[1] + left[1] * right[0]


def add(left, right):
    return left[0] + right[0], left[1] + right[1]


def plane_of(here_ref, next_ref, direction, index):
    return jnp.where(direction == 3, next_ref[index], here_ref[index])


def chosen_link(links_ref, direction):
    which = jnp.maximum(direction - 1, 0)
    resting = direction == 0

    def entry(row, column):
        at = 2 * (COLORS * row + column)
        re = links_ref[which, at : at + 1, :]
        im = links_ref[which, at + 1 : at + 2, :]
        unit = jnp.full_like(re, 1.0 if row == column else 0.0)
        return jnp.where(resting, unit, re), jnp.where(resting, jnp.zeros_like(im), im)

    return [[entry(row, column) for column in range(COLORS)] for row in range(COLORS)]


def site_matrices(combo, moves, rows, here_ref, next_ref, links_ref, shifts_ref, matrices_ref, scale):
    vectors = here_ref.shape[-2]
    direction = moves[combo, 0]
    picks = matrices_ref.shape[2]
    numbers = lax.broadcasted_iota(jnp.int32, (picks, vectors), 1)
    lane = lax.broadcasted_iota(jnp.int32, (picks, vectors), 0)
    wanted = jnp.full((picks, vectors), -1, jnp.int32)
    for i in range(rows.shape[0]):
        wanted = jnp.where(lane == i, rows[i], wanted)
    select = jnp.where(numbers == wanted, 1.0, 0.0).astype(jnp.bfloat16)

    def picked(part, color):
        return jnp.dot(
            select,
            plane_of(here_ref, next_ref, direction, (part, color)),
            preferred_element_type=jnp.float32,
        )

    stacked = jnp.concatenate(
        [picked(part, color) for color in range(COLORS) for part in range(2)], axis=0
    )
    stacked = jnp.dot(
        stacked.astype(jnp.bfloat16), in_plane(shifts_ref, direction), preferred_element_type=jnp.float32
    )
    fields = [
        tuple(stacked[at * picks : (at + 1) * picks] for at in (2 * color, 2 * color + 1))
        for color in range(COLORS)
    ]
    first, second, third = (chosen_link(links_ref, moves[combo, slot]) for slot in range(3))

    def total(terms):
        return functools.reduce(add, terms)

    left = [
        total(mul(first[a][b], fields[b]) for b in range(COLORS)) for a in range(COLORS)
    ]
    left = [(re * scale, im * scale) for re, im in left]
    for column in range(COLORS):
        after = []
        for b in range(COLORS):
            up, down = (b + 1) % COLORS, (b + 2) % COLORS
            plus = mul(third[up][column], left[down])
            minus = mul(third[down][column], left[up])
            after.append((plus[0] - minus[0], plus[1] - minus[1]))
        for row in range(COLORS):
            re, im = total(mul(second[b][row], after[b]) for b in range(COLORS))
            at = COLORS * (COLORS * column + row)
            matrices_ref[combo, at] = re + im
            matrices_ref[combo, at + 1] = re
            matrices_ref[combo, at + 2] = im


def right_operand(combo, moves, here_ref, next_ref, shifts_ref, right_ref):
    vectors, sites = here_ref.shape[-2:]
    direction = moves[combo, 2]
    shift = in_plane(shifts_ref, direction)
    kind = right_ref.dtype
    for color in range(COLORS):
        re, im = (
            jnp.dot(
                plane_of(here_ref, next_ref, direction, (part, color)),
                shift,
                preferred_element_type=jnp.float32,
            )
            for part in range(2)
        )
        of_re = slice(2 * color * sites, (2 * color + 1) * sites)
        of_im = slice((2 * color + 1) * sites, (2 * color + 2) * sites)
        right_ref[combo, :vectors, of_re] = re.astype(kind)
        right_ref[combo, vectors:, of_im] = re.astype(kind)
        right_ref[combo, :vectors, of_im] = (-im).astype(kind)
        right_ref[combo, vectors:, of_re] = im.astype(kind)


def row_block(combo, start, moves, here_ref, next_ref, shifts_ref, matrices_ref, right_ref, mid_ref, crossed_ref, out_ref):
    sites = here_ref.shape[-1]
    picks, count = out_ref.shape[1:3]
    direction = moves[combo, 1]
    rows = pl.ds(pl.multiple_of(start, TILE), count)
    block = plane_of(here_ref, next_ref, direction, (slice(None), slice(None), rows))
    half = COLORS * count
    both = jnp.dot(
        block.reshape(2 * half, sites), in_plane(shifts_ref, direction), preferred_element_type=jnp.float32
    )
    re, im = both[:half], both[half:]
    mid_ref[:half] = re
    mid_ref[half : 2 * half] = im - re
    mid_ref[2 * half :] = re + im
    result = None
    for column in range(COLORS):
        for lanes in range(sites // LANES):
            across = slice(lanes * LANES, (lanes + 1) * LANES)
            for tile in range(count // TILE):
                field = [
                    [
                        mid_ref[pl.ds(kind * half + row * count + tile * TILE, TILE), across]
                        for kind in range(3)
                    ]
                    for row in range(COLORS)
                ]
                for pick in range(picks):
                    sums = [None] * 3
                    for row in range(COLORS):
                        at = COLORS * (COLORS * column + row)
                        for kind in range(3):
                            entry = jnp.broadcast_to(
                                matrices_ref[combo, at + kind, pick : pick + 1, across], (TILE, LANES)
                            )
                            term = entry * field[row][kind]
                            sums[kind] = term if row == 0 else sums[kind] + term
                    down = slice(pick * count + tile * TILE, pick * count + (tile + 1) * TILE)
                    at = 2 * column * sites + lanes * LANES
                    crossed_ref[down, at : at + LANES] = (sums[0] - sums[2]).astype(jnp.bfloat16)
                    at += sites
                    crossed_ref[down, at : at + LANES] = (sums[0] + sums[1]).astype(jnp.bfloat16)
        deep = slice(2 * column * sites, 2 * (column + 1) * sites)
        part = lax.dot_general(
            crossed_ref[:, deep],
            right_ref[combo, :, deep],
            (((1,), (1,)), ((), ())),
            preferred_element_type=jnp.float32,
        )
        result = part if result is None else result + part
    out_ref[combo] = result.reshape(out_ref.shape[1:]).astype(out_ref.dtype)


def first_kernel(scale, starts, moves, rows, here_ref, next_ref, links_ref, shifts_ref, right_ref, matrices_ref, out_ref, mid_ref, crossed_ref):
    combos = range(out_ref.shape[0])
    for combo in combos:
        site_matrices(combo, moves, rows, here_ref, next_ref, links_ref, shifts_ref, matrices_ref, scale)
    for combo in combos:
        right_operand(combo, moves, here_ref, next_ref, shifts_ref, right_ref)
        row_block(combo, starts[0], moves, here_ref, next_ref, shifts_ref, matrices_ref, right_ref, mid_ref.at[combo], crossed_ref.at[combo], out_ref)


def later_kernel(starts, moves, here_ref, next_ref, shifts_ref, right_ref, matrices_ref, *rest):
    *outs, mid_ref, crossed_ref = rest

    def step(combo, carry):
        for number, out_ref in enumerate(outs):
            row_block(combo, starts[number], moves, here_ref, next_ref, shifts_ref, matrices_ref, right_ref, mid_ref.at[number], crossed_ref.at[number], out_ref)
        return carry

    lax.fori_loop(0, outs[0].shape[0], step, 0)


def local_work(eigenvectors, gauge_links, displacements, block_rows):
    parts, vectors, colors, planes, sites = eigenvectors.shape
    ring = lax.axis_size("site")
    me = lax.axis_index("site")
    combos, picks = displacements.shape[0], block_rows.shape[0]
    count = vectors // ring
    scale = 1.0 / math.sqrt(24.0 * planes * ring * sites)
    here = jnp.transpose(eigenvectors, (0, 2, 3, 1, 4)).reshape(parts, colors, vectors, sites)
    after = shifted(here, "site", -1)
    links = jnp.transpose(gauge_links, (1, 2, 3, 0, 4, 5)).astype(jnp.float32)
    links = links.reshape(COLORS, colors * colors * parts, sites)
    shifts = shift_matrices(sites, LX)

    def chunk(kind):
        return jax.ShapeDtypeStruct((combos, picks, count, 2 * vectors), kind)

    def starts(owners):
        return jnp.stack([owner * count for owner in owners]).astype(jnp.int32)

    smem = pl.BlockSpec(memory_space=pltpu.SMEM)
    vmem = pl.BlockSpec(memory_space=pltpu.VMEM)

    def scratch(blocks):
        return [
            pltpu.VMEM((blocks, 3 * colors * count, sites), jnp.float32),
            pltpu.VMEM((blocks, picks * count, parts * colors * sites), jnp.bfloat16),
        ]

    folded = ring == 4
    if folded:
        owners = [ring - 1 - me, lax.rem(me + 2, ring), me + 1 - 2 * lax.rem(me, 2), me]
    else:
        owners = [lax.rem(me + offset, ring) for offset in range(1, ring + 1)]
    right, matrices, sent = pl.pallas_call(
        functools.partial(first_kernel, scale),
        out_shape=(
            jax.ShapeDtypeStruct((combos, 2 * vectors, parts * colors * sites), jnp.bfloat16),
            jax.ShapeDtypeStruct((combos, 3 * colors * colors, SUBLANES, sites), jnp.float32),
            chunk(jnp.bfloat16),
        ),
        in_specs=[smem, smem, smem, vmem, vmem, vmem, vmem],
        out_specs=(vmem, vmem, vmem),
        scratch_shapes=scratch(combos),
        compiler_params=pltpu.CompilerParams(vmem_limit_bytes=VMEM_BYTES),
        name="first",
    )(starts(owners[:1]), displacements, block_rows, here, after, links, shifts)
    others = pl.pallas_call(
        later_kernel,
        out_shape=tuple(chunk(jnp.bfloat16) for _ in owners[1:-1]) + (chunk(jnp.float32),),
        in_specs=[smem, smem, vmem, vmem, vmem, vmem, vmem],
        out_specs=(vmem,) * (ring - 1),
        scratch_shapes=scratch(ring - 1),
        compiler_params=pltpu.CompilerParams(vmem_limit_bytes=VMEM_BYTES),
        cost_estimate=pl.CostEstimate(flops=3_000_000_000, bytes_accessed=8_000_000, transcendentals=0),
        name="later",
    )(starts(owners[1:]), displacements, here, after, shifts, right, matrices)
    if not folded:
        blocks = [sent, *others[:-1]]
        arrived = [shifted(block, "site", offset + 1) for offset, block in enumerate(blocks)]
        return functools.reduce(lambda total, block: total + block.astype(jnp.float32), arrived, others[-1])
    last = ring - 1
    passed = lax.ppermute(sent, "site", [(0, 1), (last, last - 1)])
    near = lax.ppermute(sent, "site", [(1, 2), (2, 1)])
    paired = lax.ppermute(others[1], "site", [(0, 1), (1, 0), (2, 3), (3, 2)])
    far = shifted(others[0] + passed, "site", 2)
    held = others[2] + near.astype(jnp.float32) + paired.astype(jnp.float32)
    held = lax.optimization_barrier(held)
    return held + far.astype(jnp.float32)


def solution(mesh):
    return jax.shard_map(
        local_work,
        mesh=mesh,
        in_specs=(
            P("ta", None, None, "site", None),
            P("ta", None, None, None, "site", None),
            P(),
            P(),
        ),
        out_specs=P("ta", None, "site", None),
        check_vma=False,
    )
```

```python
import functools
import math

import jax
import jax.numpy as jnp
from jax import lax
from jax.experimental import pallas as pl
from jax.experimental.pallas import tpu as pltpu
from jax.sharding import PartitionSpec as P


LX = 16
COLORS = 3
TILE = 16
LANES = 128
SUBLANES = 8
VMEM_BYTES = 16 * 2**20


def shifted(block, axis, distance):
    count = lax.axis_size(axis)
    return lax.ppermute(block, axis, [(i, (i + distance) % count) for i in range(count)])


def shift_matrices(sites, width_x):
    source = lax.broadcasted_iota(jnp.int32, (COLORS, sites, sites), 1)
    target = lax.broadcasted_iota(jnp.int32, (COLORS, sites, sites), 2)
    direction = lax.broadcasted_iota(jnp.int32, (COLORS, sites, sites), 0)
    column = lax.rem(target, width_x)
    along_x = target - column + lax.rem(column + 1, width_x)
    along_y = lax.rem(target + width_x, sites)
    neighbour = jnp.where(direction == 1, along_x, jnp.where(direction == 2, along_y, target))
    return jnp.where(source == neighbour, 1.0, 0.0).astype(jnp.bfloat16)


def in_plane(shifts_ref, direction):
    return shifts_ref[jnp.where(direction == 3, 0, direction)]


def mul(left, right):
    return left[0] * right[0] - left[1] * right[1], left[0] * right[1] + left[1] * right[0]


def add(left, right):
    return left[0] + right[0], left[1] + right[1]


def plane_of(here_ref, next_ref, direction, index):
    return jnp.where(direction == 3, next_ref[index], here_ref[index])


def chosen_link(links_ref, direction):
    which = jnp.maximum(direction - 1, 0)
    resting = direction == 0

    def entry(row, column):
        at = 2 * (COLORS * row + column)
        re = links_ref[which, at : at + 1, :]
        im = links_ref[which, at + 1 : at + 2, :]
        unit = jnp.full_like(re, 1.0 if row == column else 0.0)
        return jnp.where(resting, unit, re), jnp.where(resting, jnp.zeros_like(im), im)

    return [[entry(row, column) for column in range(COLORS)] for row in range(COLORS)]


def site_matrices(combo, moves, rows, here_ref, next_ref, links_ref, shifts_ref, matrices_ref, scale):
    vectors = here_ref.shape[-2]
    direction = moves[combo, 0]
    kept, picks = matrices_ref.shape[2], SUBLANES
    numbers = lax.broadcasted_iota(jnp.int32, (picks, vectors), 1)
    lane = lax.broadcasted_iota(jnp.int32, (picks, vectors), 0)
    wanted = jnp.full((picks, vectors), -1, jnp.int32)
    for i in range(rows.shape[0]):
        wanted = jnp.where(lane == i, rows[i], wanted)
    select = jnp.where(numbers == wanted, 1.0, 0.0).astype(jnp.bfloat16)

    def picked(part, color):
        return jnp.dot(
            select,
            plane_of(here_ref, next_ref, direction, (part, color)),
            preferred_element_type=jnp.float32,
        )

    stacked = jnp.concatenate(
        [picked(part, color) for color in range(COLORS) for part in range(2)], axis=0
    )
    stacked = jnp.dot(
        stacked.astype(jnp.bfloat16), in_plane(shifts_ref, direction), preferred_element_type=jnp.float32
    )
    fields = [
        tuple(stacked[at * picks : (at + 1) * picks] for at in (2 * color, 2 * color + 1))
        for color in range(COLORS)
    ]
    first, second, third = (chosen_link(links_ref, moves[combo, slot]) for slot in range(3))

    def total(terms):
        return functools.reduce(add, terms)

    left = [
        total(mul(first[a][b], fields[b]) for b in range(COLORS)) for a in range(COLORS)
    ]
    left = [(re * scale, im * scale) for re, im in left]
    for column in range(COLORS):
        after = []
        for b in range(COLORS):
            up, down = (b + 1) % COLORS, (b + 2) % COLORS
            plus = mul(third[up][column], left[down])
            minus = mul(third[down][column], left[up])
            after.append((plus[0] - minus[0], plus[1] - minus[1]))
        for row in range(COLORS):
            re, im = total(mul(second[b][row], after[b]) for b in range(COLORS))
            at = COLORS * (COLORS * column + row)
            matrices_ref[combo, at] = (re + im)[:kept]
            matrices_ref[combo, at + 1] = re[:kept]
            matrices_ref[combo, at + 2] = im[:kept]


def right_operand(combo, moves, here_ref, next_ref, shifts_ref, right_ref):
    vectors, sites = here_ref.shape[-2:]
    direction = moves[combo, 2]
    shift = in_plane(shifts_ref, direction)
    for color in range(COLORS):
        for part in range(2):
            field = jnp.dot(
                plane_of(here_ref, next_ref, direction, (part, color)),
                shift,
                preferred_element_type=jnp.float32,
            )
            right_ref[
                combo, part * vectors : (part + 1) * vectors, color * sites : (color + 1) * sites
            ] = field.astype(right_ref.dtype)


def turn(right_ref, turned_ref):
    vectors = right_ref.shape[1] // 2
    for combo in range(right_ref.shape[0]):
        turned_ref[combo, :vectors] = -right_ref[combo, vectors:]
        turned_ref[combo, vectors:] = right_ref[combo, :vectors]


def row_block(combo, start, moves, here_ref, next_ref, shifts_ref, matrices_ref, right_ref, turned_ref, mid_ref, crossed_ref, out_ref):
    sites = here_ref.shape[-1]
    picks, count = out_ref.shape[1:3]
    direction = moves[combo, 1]
    rows = pl.ds(pl.multiple_of(start, TILE), count)
    block = plane_of(here_ref, next_ref, direction, (slice(None), slice(None), rows))
    half = COLORS * count
    both = jnp.dot(
        block.reshape(2 * half, sites), in_plane(shifts_ref, direction), preferred_element_type=jnp.float32
    )
    re, im = both[:half], both[half:]
    mid_ref[:half] = re
    mid_ref[half : 2 * half] = im - re
    mid_ref[2 * half :] = re + im
    result = None
    for column in range(COLORS):
        for lanes in range(sites // LANES):
            across = slice(lanes * LANES, (lanes + 1) * LANES)
            for tile in range(count // TILE):
                field = [
                    [
                        mid_ref[pl.ds(kind * half + row * count + tile * TILE, TILE), across]
                        for kind in range(3)
                    ]
                    for row in range(COLORS)
                ]
                for pick in range(picks):
                    sums = [None] * 3
                    for row in range(COLORS):
                        at = COLORS * (COLORS * column + row)
                        for kind in range(3):
                            entry = jnp.broadcast_to(
                                matrices_ref[combo, at + kind, pick : pick + 1, across], (TILE, LANES)
                            )
                            term = entry * field[row][kind]
                            sums[kind] = term if row == 0 else sums[kind] + term
                    down = slice(pick * count + tile * TILE, pick * count + (tile + 1) * TILE)
                    at = 2 * column * sites + lanes * LANES
                    crossed_ref[down, at : at + LANES] = (sums[0] - sums[2]).astype(jnp.bfloat16)
                    at += sites
                    crossed_ref[down, at : at + LANES] = (sums[0] + sums[1]).astype(jnp.bfloat16)
        deep = slice(2 * column * sites, 2 * (column + 1) * sites)
        wide = slice(column * sites, (column + 1) * sites)
        part = lax.dot_general(
            crossed_ref[:, deep],
            jnp.concatenate([right_ref[combo, :, wide], turned_ref[combo, :, wide]], axis=1),
            (((1,), (1,)), ((), ())),
            preferred_element_type=jnp.float32,
        )
        result = part if result is None else result + part
    out_ref[combo] = result.reshape(out_ref.shape[1:]).astype(out_ref.dtype)


def moves_of(meta, layout):
    ring, combos = layout

    class Moves:
        def __getitem__(self, key):
            combo, slot = key
            return meta[ring + 3 * combo + slot]

    class Rows:
        shape = (meta.shape[0] - ring - 3 * combos,)

        def __getitem__(self, i):
            return meta[ring + 3 * combos + i]

    return Moves(), Rows()


def prepare(of_next, layout, scale, meta, here_ref, next_ref, links_ref, shifts_ref, right_ref, matrices_ref):
    moves, rows = moves_of(meta, layout)
    for combo in range(layout[1]):

        @pl.when((moves[combo, 0] == 3) == of_next)
        def _(combo=combo):
            site_matrices(combo, moves, rows, here_ref, next_ref, links_ref, shifts_ref, matrices_ref, scale)

        @pl.when((moves[combo, 2] == 3) == of_next)
        def _(combo=combo):
            right_operand(combo, moves, here_ref, next_ref, shifts_ref, right_ref)


def early_kernel(layout, scale, meta, here_ref, links_ref, shifts_ref, right_ref, matrices_ref, copy_ref):
    copy_ref[...] = here_ref[...]
    prepare(False, layout, scale, meta, here_ref, here_ref, links_ref, shifts_ref, right_ref, matrices_ref)


def first_kernel(layout, scale, meta, here_ref, next_ref, links_ref, shifts_ref, right_in, matrices_in, right_ref, matrices_ref, out_ref, turned_ref, mid_ref, crossed_ref):
    prepare(True, layout, scale, meta, here_ref, next_ref, links_ref, shifts_ref, right_ref, matrices_ref)
    turn(right_ref, turned_ref)
    moves, _ = moves_of(meta, layout)
    for combo in range(layout[1]):
        row_block(combo, meta[0], moves, here_ref, next_ref, shifts_ref, matrices_ref, right_ref, turned_ref, mid_ref.at[combo], crossed_ref.at[combo], out_ref)


def block_kernel(number, layout, meta, here_ref, next_ref, shifts_ref, right_ref, matrices_ref, out_ref, turned_ref, mid_ref, crossed_ref):
    turn(right_ref, turned_ref)
    moves, _ = moves_of(meta, layout)
    for combo in range(layout[1]):
        row_block(combo, meta[number], moves, here_ref, next_ref, shifts_ref, matrices_ref, right_ref, turned_ref, mid_ref.at[combo], crossed_ref.at[combo], out_ref)


def local_work(eigenvectors, gauge_links, displacements, block_rows):
    parts, vectors, colors, planes, sites = eigenvectors.shape
    ring = lax.axis_size("site")
    me = lax.axis_index("site")
    combos, picks = displacements.shape[0], block_rows.shape[0]
    layout = (ring, combos)
    count = vectors // ring
    scale = 1.0 / math.sqrt(24.0 * planes * ring * sites)
    here = jnp.transpose(eigenvectors, (0, 2, 3, 1, 4)).reshape(parts, colors, vectors, sites)
    after = shifted(here, "site", -1)
    links = jnp.transpose(gauge_links, (1, 2, 3, 0, 4, 5)).astype(jnp.float32)
    links = links.reshape(COLORS, colors * colors * parts, sites)
    shifts = shift_matrices(sites, LX)
    last = ring - 1
    folded = ring == 4
    if folded:
        odd = lax.rem(me, 2)
        owners = [last * (1 - odd), 1 + odd, lax.rem(me + 2, ring), me]
    else:
        owners = [lax.rem(me + offset, ring) for offset in range(1, ring + 1)]
    meta = jnp.concatenate(
        [jnp.stack(owners) * count, displacements.reshape(-1), block_rows]
    ).astype(jnp.int32)

    smem = pl.BlockSpec(memory_space=pltpu.SMEM)
    vmem = pl.BlockSpec(memory_space=pltpu.VMEM)
    right = jax.ShapeDtypeStruct((combos, parts * vectors, colors * sites), jnp.bfloat16)
    matrices = jax.ShapeDtypeStruct((combos, 3 * colors * colors, picks, sites), jnp.float32)
    scratch = [
        pltpu.VMEM(right.shape, right.dtype),
        pltpu.VMEM((combos, 3 * colors * count, sites), jnp.float32),
        pltpu.VMEM((combos, picks * count, parts * colors * sites), jnp.bfloat16),
    ]
    params = pltpu.CompilerParams(vmem_limit_bytes=VMEM_BYTES)

    def chunk(kind):
        return jax.ShapeDtypeStruct((combos, picks, count, 2 * vectors), kind)

    right, matrices, here = pl.pallas_call(
        functools.partial(early_kernel, layout, scale),
        out_shape=(right, matrices, jax.ShapeDtypeStruct(here.shape, here.dtype)),
        in_specs=[smem, vmem, vmem, vmem],
        out_specs=(vmem, vmem, vmem),
        compiler_params=params,
        cost_estimate=pl.CostEstimate(flops=500_000_000, bytes_accessed=4_000_000, transcendentals=0),
        name="early",
    )(meta, here, links, shifts)
    right, matrices, sent = pl.pallas_call(
        functools.partial(first_kernel, layout, scale),
        out_shape=(
            jax.ShapeDtypeStruct(right.shape, right.dtype),
            jax.ShapeDtypeStruct(matrices.shape, matrices.dtype),
            chunk(jnp.bfloat16),
        ),
        in_specs=[smem, vmem, vmem, vmem, vmem, vmem, vmem],
        out_specs=(vmem, vmem, vmem),
        input_output_aliases={5: 0, 6: 1},
        scratch_shapes=scratch,
        compiler_params=params,
        name="first",
    )(meta, here, after, links, shifts, right, matrices)
    blocks = [sent]
    for number in range(1, ring):
        blocks.append(
            pl.pallas_call(
                functools.partial(block_kernel, number, layout),
                out_shape=chunk(jnp.float32 if number == last else jnp.bfloat16),
                in_specs=[smem, vmem, vmem, vmem, vmem, vmem],
                out_specs=vmem,
                scratch_shapes=scratch,
                compiler_params=params,
                cost_estimate=pl.CostEstimate(flops=1_000_000_000, bytes_accessed=4_000_000, transcendentals=0),
            )(meta, here, after, shifts, right, matrices)
        )
    own = blocks.pop()
    if not folded:
        arrived = [shifted(block, "site", offset + 1) for offset, block in enumerate(blocks)]
        return functools.reduce(lambda total, block: total + block.astype(jnp.float32), arrived, own)
    paired = lax.ppermute(blocks[0], "site", [(0, 1), (1, 0), (2, 3), (3, 2)])
    near = lax.ppermute(blocks[1], "site", [(1, 2), (2, 1)])
    inner = (me > 0) & (me < last)
    far = shifted(blocks[2] + jnp.where(inner, paired, jnp.zeros_like(paired)), "site", 2)
    inward = lax.ppermute(blocks[1], "site", [(0, 1), (3, 2)])
    held = own + near.astype(jnp.float32) + inward.astype(jnp.float32)
    held = held + jnp.where(inner, jnp.zeros_like(paired), paired).astype(jnp.float32)
    held = lax.optimization_barrier(held)
    return held + far.astype(jnp.float32)


def solution(mesh):
    step = jax.shard_map(
        local_work,
        mesh=mesh,
        in_specs=(
            P("ta", None, None, "site", None),
            P("ta", None, None, None, "site", None),
            P(),
            P(),
        ),
        out_specs=P("ta", None, "site", None),
        check_vma=False,
    )
    if mesh.shape["site"] != 4:
        return step
    return step
```

```python
import functools
import math

import jax
import jax.numpy as jnp
from jax import lax
from jax.experimental import pallas as pl
from jax.experimental.pallas import tpu as pltpu
from jax.sharding import PartitionSpec as P


LX = 16
COLORS = 3
TILE = 16
LANES = 128
SUBLANES = 8
VMEM_BYTES = 16 * 2**20


def shifted(block, axis, distance):
    count = lax.axis_size(axis)
    return lax.ppermute(block, axis, [(i, (i + distance) % count) for i in range(count)])


def shift_matrices(sites, width_x):
    source = lax.broadcasted_iota(jnp.int32, (COLORS, sites, sites), 1)
    target = lax.broadcasted_iota(jnp.int32, (COLORS, sites, sites), 2)
    direction = lax.broadcasted_iota(jnp.int32, (COLORS, sites, sites), 0)
    column = lax.rem(target, width_x)
    along_x = target - column + lax.rem(column + 1, width_x)
    along_y = lax.rem(target + width_x, sites)
    neighbour = jnp.where(direction == 1, along_x, jnp.where(direction == 2, along_y, target))
    return jnp.where(source == neighbour, 1.0, 0.0).astype(jnp.bfloat16)


def in_plane(shifts_ref, direction):
    return shifts_ref[jnp.where(direction == 3, 0, direction)]


def mul(left, right):
    return left[0] * right[0] - left[1] * right[1], left[0] * right[1] + left[1] * right[0]


def add(left, right):
    return left[0] + right[0], left[1] + right[1]


def plane_of(here_ref, next_ref, direction, index):
    return jnp.where(direction == 3, next_ref[index], here_ref[index])


def chosen_link(links_ref, direction):
    which = jnp.maximum(direction - 1, 0)
    resting = direction == 0

    def entry(row, column):
        at = 2 * (COLORS * row + column)
        re = links_ref[which, at : at + 1, :]
        im = links_ref[which, at + 1 : at + 2, :]
        unit = jnp.full_like(re, 1.0 if row == column else 0.0)
        return jnp.where(resting, unit, re), jnp.where(resting, jnp.zeros_like(im), im)

    return [[entry(row, column) for column in range(COLORS)] for row in range(COLORS)]


def site_matrices(combo, moves, rows, here_ref, next_ref, links_ref, shifts_ref, matrices_ref, scale):
    vectors = here_ref.shape[-2]
    direction = moves[combo, 0]
    kept, picks = matrices_ref.shape[2], SUBLANES
    numbers = lax.broadcasted_iota(jnp.int32, (picks, vectors), 1)
    lane = lax.broadcasted_iota(jnp.int32, (picks, vectors), 0)
    wanted = jnp.full((picks, vectors), -1, jnp.int32)
    for i in range(rows.shape[0]):
        wanted = jnp.where(lane == i, rows[i], wanted)
    select = jnp.where(numbers == wanted, 1.0, 0.0).astype(jnp.bfloat16)

    def picked(part, color):
        return jnp.dot(
            select,
            plane_of(here_ref, next_ref, direction, (part, color)),
            preferred_element_type=jnp.float32,
        )

    stacked = jnp.concatenate(
        [picked(part, color) for color in range(COLORS) for part in range(2)], axis=0
    )
    stacked = jnp.dot(
        stacked.astype(jnp.bfloat16), in_plane(shifts_ref, direction), preferred_element_type=jnp.float32
    )
    fields = [
        tuple(stacked[at * picks : (at + 1) * picks] for at in (2 * color, 2 * color + 1))
        for color in range(COLORS)
    ]
    first, second, third = (chosen_link(links_ref, moves[combo, slot]) for slot in range(3))

    def total(terms):
        return functools.reduce(add, terms)

    left = [
        total(mul(first[a][b], fields[b]) for b in range(COLORS)) for a in range(COLORS)
    ]
    left = [(re * scale, im * scale) for re, im in left]
    for column in range(COLORS):
        after = []
        for b in range(COLORS):
            up, down = (b + 1) % COLORS, (b + 2) % COLORS
            plus = mul(third[up][column], left[down])
            minus = mul(third[down][column], left[up])
            after.append((plus[0] - minus[0], plus[1] - minus[1]))
        for row in range(COLORS):
            re, im = total(mul(second[b][row], after[b]) for b in range(COLORS))
            at = COLORS * (COLORS * column + row)
            matrices_ref[combo, at] = (re + im)[:kept]
            matrices_ref[combo, at + 1] = re[:kept]
            matrices_ref[combo, at + 2] = im[:kept]


def right_operand(combo, moves, here_ref, next_ref, shifts_ref, right_ref):
    vectors, sites = here_ref.shape[-2:]
    direction = moves[combo, 2]
    shift = in_plane(shifts_ref, direction)
    for color in range(COLORS):
        for part in range(2):
            field = jnp.dot(
                plane_of(here_ref, next_ref, direction, (part, color)),
                shift,
                preferred_element_type=jnp.float32,
            )
            right_ref[
                combo, part * vectors : (part + 1) * vectors, color * sites : (color + 1) * sites
            ] = field.astype(right_ref.dtype)


def turn(right_ref, turned_ref):
    vectors = right_ref.shape[1] // 2
    for combo in range(right_ref.shape[0]):
        turned_ref[combo, :vectors] = -right_ref[combo, vectors:]
        turned_ref[combo, vectors:] = right_ref[combo, :vectors]


def row_block(combo, start, moves, here_ref, next_ref, shifts_ref, matrices_ref, right_ref, turned_ref, mid_ref, crossed_ref, out_ref):
    sites = here_ref.shape[-1]
    picks, count = out_ref.shape[1:3]
    direction = moves[combo, 1]
    rows = pl.ds(pl.multiple_of(start, TILE), count)
    block = plane_of(here_ref, next_ref, direction, (slice(None), slice(None), rows))
    half = COLORS * count
    both = jnp.dot(
        block.reshape(2 * half, sites), in_plane(shifts_ref, direction), preferred_element_type=jnp.float32
    )
    re, im = both[:half], both[half:]
    mid_ref[:half] = re
    mid_ref[half : 2 * half] = im - re
    mid_ref[2 * half :] = re + im
    result = None
    for column in range(COLORS):
        for lanes in range(sites // LANES):
            across = slice(lanes * LANES, (lanes + 1) * LANES)
            for tile in range(count // TILE):
                field = [
                    [
                        mid_ref[pl.ds(kind * half + row * count + tile * TILE, TILE), across]
                        for kind in range(3)
                    ]
                    for row in range(COLORS)
                ]
                for pick in range(picks):
                    sums = [None] * 3
                    for row in range(COLORS):
                        at = COLORS * (COLORS * column + row)
                        for kind in range(3):
                            entry = jnp.broadcast_to(
                                matrices_ref[combo, at + kind, pick : pick + 1, across], (TILE, LANES)
                            )
                            term = entry * field[row][kind]
                            sums[kind] = term if row == 0 else sums[kind] + term
                    down = slice(pick * count + tile * TILE, pick * count + (tile + 1) * TILE)
                    at = 2 * column * sites + lanes * LANES
                    crossed_ref[down, at : at + LANES] = (sums[0] - sums[2]).astype(jnp.bfloat16)
                    at += sites
                    crossed_ref[down, at : at + LANES] = (sums[0] + sums[1]).astype(jnp.bfloat16)
        deep = slice(2 * column * sites, 2 * (column + 1) * sites)
        wide = slice(column * sites, (column + 1) * sites)
        part = lax.dot_general(
            crossed_ref[:, deep],
            jnp.concatenate([right_ref[combo, :, wide], turned_ref[combo, :, wide]], axis=1),
            (((1,), (1,)), ((), ())),
            preferred_element_type=jnp.float32,
        )
        result = part if result is None else result + part
    out_ref[combo] = result.reshape(out_ref.shape[1:]).astype(out_ref.dtype)


def moves_of(meta, layout):
    ring, combos = layout

    class Moves:
        def __getitem__(self, key):
            combo, slot = key
            return meta[ring + 3 * combo + slot]

    class Rows:
        shape = (meta.shape[0] - ring - 3 * combos,)

        def __getitem__(self, i):
            return meta[ring + 3 * combos + i]

    return Moves(), Rows()


def prepare(of_next, layout, scale, meta, here_ref, next_ref, links_ref, shifts_ref, right_ref, matrices_ref):
    moves, rows = moves_of(meta, layout)
    for combo in range(layout[1]):

        @pl.when((moves[combo, 0] == 3) == of_next)
        def _(combo=combo):
            site_matrices(combo, moves, rows, here_ref, next_ref, links_ref, shifts_ref, matrices_ref, scale)

        @pl.when((moves[combo, 2] == 3) == of_next)
        def _(combo=combo):
            right_operand(combo, moves, here_ref, next_ref, shifts_ref, right_ref)


def early_kernel(layout, scale, meta, here_ref, links_ref, shifts_ref, right_ref, matrices_ref, copy_ref):
    copy_ref[...] = here_ref[...]
    prepare(False, layout, scale, meta, here_ref, here_ref, links_ref, shifts_ref, right_ref, matrices_ref)


def first_kernel(layout, scale, meta, here_ref, next_ref, links_ref, shifts_ref, right_in, matrices_in, right_ref, matrices_ref, out_ref, turned_ref, mid_ref, crossed_ref):
    prepare(True, layout, scale, meta, here_ref, next_ref, links_ref, shifts_ref, right_ref, matrices_ref)
    turn(right_ref, turned_ref)
    moves, _ = moves_of(meta, layout)
    for combo in range(layout[1]):
        row_block(combo, meta[0], moves, here_ref, next_ref, shifts_ref, matrices_ref, right_ref, turned_ref, mid_ref.at[combo], crossed_ref.at[combo], out_ref)


def block_kernel(number, layout, meta, here_ref, next_ref, shifts_ref, right_ref, matrices_ref, out_ref, turned_ref, mid_ref, crossed_ref):
    turn(right_ref, turned_ref)
    moves, _ = moves_of(meta, layout)
    for combo in range(layout[1]):
        row_block(combo, meta[number], moves, here_ref, next_ref, shifts_ref, matrices_ref, right_ref, turned_ref, mid_ref.at[combo], crossed_ref.at[combo], out_ref)


def local_work(eigenvectors, gauge_links, displacements, block_rows):
    parts, vectors, colors, planes, sites = eigenvectors.shape
    ring = lax.axis_size("site")
    me = lax.axis_index("site")
    combos, picks = displacements.shape[0], block_rows.shape[0]
    layout = (ring, combos)
    count = vectors // ring
    scale = 1.0 / math.sqrt(24.0 * planes * ring * sites)
    here = jnp.transpose(eigenvectors, (0, 2, 3, 1, 4)).reshape(parts, colors, vectors, sites)
    after = shifted(here, "site", -1)
    links = jnp.transpose(gauge_links, (1, 2, 3, 0, 4, 5)).astype(jnp.float32)
    links = links.reshape(COLORS, colors * colors * parts, sites)
    shifts = shift_matrices(sites, LX)
    last = ring - 1
    folded = ring == 4
    if folded:
        owners = [last - me, lax.rem(me + 2, ring), me + 1 - 2 * lax.rem(me, 2), me]
    else:
        owners = [lax.rem(me + offset, ring) for offset in range(1, ring + 1)]
    meta = jnp.concatenate(
        [jnp.stack(owners) * count, displacements.reshape(-1), block_rows]
    ).astype(jnp.int32)

    smem = pl.BlockSpec(memory_space=pltpu.SMEM)
    vmem = pl.BlockSpec(memory_space=pltpu.VMEM)
    right = jax.ShapeDtypeStruct((combos, parts * vectors, colors * sites), jnp.bfloat16)
    matrices = jax.ShapeDtypeStruct((combos, 3 * colors * colors, picks, sites), jnp.float32)
    scratch = [
        pltpu.VMEM(right.shape, right.dtype),
        pltpu.VMEM((combos, 3 * colors * count, sites), jnp.float32),
        pltpu.VMEM((combos, picks * count, parts * colors * sites), jnp.bfloat16),
    ]
    params = pltpu.CompilerParams(vmem_limit_bytes=VMEM_BYTES)

    def chunk(kind):
        return jax.ShapeDtypeStruct((combos, picks, count, 2 * vectors), kind)

    right, matrices, here = pl.pallas_call(
        functools.partial(early_kernel, layout, scale),
        out_shape=(right, matrices, jax.ShapeDtypeStruct(here.shape, here.dtype)),
        in_specs=[smem, vmem, vmem, vmem],
        out_specs=(vmem, vmem, vmem),
        compiler_params=params,
        cost_estimate=pl.CostEstimate(flops=500_000_000, bytes_accessed=4_000_000, transcendentals=0),
        name="early",
    )(meta, here, links, shifts)
    right, matrices, sent = pl.pallas_call(
        functools.partial(first_kernel, layout, scale),
        out_shape=(
            jax.ShapeDtypeStruct(right.shape, right.dtype),
            jax.ShapeDtypeStruct(matrices.shape, matrices.dtype),
            chunk(jnp.bfloat16),
        ),
        in_specs=[smem, vmem, vmem, vmem, vmem, vmem, vmem],
        out_specs=(vmem, vmem, vmem),
        input_output_aliases={5: 0, 6: 1},
        scratch_shapes=scratch,
        compiler_params=params,
        name="first",
    )(meta, here, after, links, shifts, right, matrices)
    blocks = [sent]
    for number in range(1, ring):
        blocks.append(
            pl.pallas_call(
                functools.partial(block_kernel, number, layout),
                out_shape=chunk(jnp.float32 if number == last else jnp.bfloat16),
                in_specs=[smem, vmem, vmem, vmem, vmem, vmem],
                out_specs=vmem,
                scratch_shapes=scratch,
                compiler_params=params,
                cost_estimate=pl.CostEstimate(flops=1_000_000_000, bytes_accessed=4_000_000, transcendentals=0),
            )(meta, here, after, shifts, right, matrices)
        )
    own = blocks.pop()
    if not folded:
        arrived = [shifted(block, "site", offset + 1) for offset, block in enumerate(blocks)]
        return functools.reduce(lambda total, block: total + block.astype(jnp.float32), arrived, own)
    near = lax.ppermute(blocks[0], "site", [(1, 2), (2, 1)])
    passed = lax.ppermute(blocks[0], "site", [(0, 1), (3, 2)])
    far = shifted(blocks[1] + passed, "site", 2)
    paired = lax.ppermute(blocks[2], "site", [(0, 1), (1, 0), (2, 3), (3, 2)])
    held = own + near.astype(jnp.float32) + paired.astype(jnp.float32)
    held = lax.optimization_barrier(held)
    return held + far.astype(jnp.float32)


def solution(mesh):
    step = jax.shard_map(
        local_work,
        mesh=mesh,
        in_specs=(
            P("ta", None, None, "site", None),
            P("ta", None, None, None, "site", None),
            P(),
            P(),
        ),
        out_specs=P("ta", None, "site", None),
        check_vma=False,
    )
    if mesh.shape["site"] != 4:
        return step
    return step
```

```python
import functools
import math

import jax
import jax.numpy as jnp
from jax import lax
from jax.experimental import pallas as pl
from jax.experimental.pallas import tpu as pltpu
from jax.sharding import PartitionSpec as P


LX = 16
COLORS = 3
TILE = 16
LANES = 128
SUBLANES = 8
VMEM_BYTES = 16 * 2**20


def shifted(block, axis, distance):
    count = lax.axis_size(axis)
    return lax.ppermute(block, axis, [(i, (i + distance) % count) for i in range(count)])


def shift_matrices(sites, width_x):
    source = lax.broadcasted_iota(jnp.int32, (COLORS, sites, sites), 1)
    target = lax.broadcasted_iota(jnp.int32, (COLORS, sites, sites), 2)
    direction = lax.broadcasted_iota(jnp.int32, (COLORS, sites, sites), 0)
    column = lax.rem(target, width_x)
    along_x = target - column + lax.rem(column + 1, width_x)
    along_y = lax.rem(target + width_x, sites)
    neighbour = jnp.where(direction == 1, along_x, jnp.where(direction == 2, along_y, target))
    return jnp.where(source == neighbour, 1.0, 0.0).astype(jnp.bfloat16)


def in_plane(shifts_ref, direction):
    return shifts_ref[jnp.where(direction == 3, 0, direction)]


def mul(left, right):
    return left[0] * right[0] - left[1] * right[1], left[0] * right[1] + left[1] * right[0]


def add(left, right):
    return left[0] + right[0], left[1] + right[1]


def plane_of(here_ref, next_ref, direction, index):
    return jnp.where(direction == 3, next_ref[index], here_ref[index])


def chosen_link(links_ref, direction):
    which = jnp.maximum(direction - 1, 0)
    resting = direction == 0

    def entry(row, column):
        at = 2 * (COLORS * row + column)
        re = links_ref[which, at : at + 1, :]
        im = links_ref[which, at + 1 : at + 2, :]
        unit = jnp.full_like(re, 1.0 if row == column else 0.0)
        return jnp.where(resting, unit, re), jnp.where(resting, jnp.zeros_like(im), im)

    return [[entry(row, column) for column in range(COLORS)] for row in range(COLORS)]


def site_matrices(combo, moves, rows, here_ref, next_ref, links_ref, shifts_ref, matrices_ref, scale):
    vectors = here_ref.shape[-2]
    direction = moves[combo, 0]
    kept, picks = matrices_ref.shape[2], SUBLANES
    numbers = lax.broadcasted_iota(jnp.int32, (picks, vectors), 1)
    lane = lax.broadcasted_iota(jnp.int32, (picks, vectors), 0)
    wanted = jnp.full((picks, vectors), -1, jnp.int32)
    for i in range(rows.shape[0]):
        wanted = jnp.where(lane == i, rows[i], wanted)
    select = jnp.where(numbers == wanted, 1.0, 0.0).astype(jnp.bfloat16)

    def picked(part, color):
        return jnp.dot(
            select,
            plane_of(here_ref, next_ref, direction, (part, color)),
            preferred_element_type=jnp.float32,
        )

    stacked = jnp.concatenate(
        [picked(part, color) for color in range(COLORS) for part in range(2)], axis=0
    )
    stacked = jnp.dot(
        stacked.astype(jnp.bfloat16), in_plane(shifts_ref, direction), preferred_element_type=jnp.float32
    )
    fields = [
        tuple(stacked[at * picks : (at + 1) * picks] for at in (2 * color, 2 * color + 1))
        for color in range(COLORS)
    ]
    first, second, third = (chosen_link(links_ref, moves[combo, slot]) for slot in range(3))

    def total(terms):
        return functools.reduce(add, terms)

    left = [
        total(mul(first[a][b], fields[b]) for b in range(COLORS)) for a in range(COLORS)
    ]
    left = [(re * scale, im * scale) for re, im in left]
    for column in range(COLORS):
        after = []
        for b in range(COLORS):
            up, down = (b + 1) % COLORS, (b + 2) % COLORS
            plus = mul(third[up][column], left[down])
            minus = mul(third[down][column], left[up])
            after.append((plus[0] - minus[0], plus[1] - minus[1]))
        for row in range(COLORS):
            re, im = total(mul(second[b][row], after[b]) for b in range(COLORS))
            at = COLORS * (COLORS * column + row)
            matrices_ref[combo, at] = (re + im)[:kept]
            matrices_ref[combo, at + 1] = re[:kept]
            matrices_ref[combo, at + 2] = im[:kept]


def right_operand(combo, moves, here_ref, next_ref, shifts_ref, right_ref):
    vectors, sites = here_ref.shape[-2:]
    direction = moves[combo, 2]
    shift = in_plane(shifts_ref, direction)
    for color in range(COLORS):
        for part in range(2):
            field = jnp.dot(
                plane_of(here_ref, next_ref, direction, (part, color)),
                shift,
                preferred_element_type=jnp.float32,
            )
            right_ref[
                combo, part * vectors : (part + 1) * vectors, color * sites : (color + 1) * sites
            ] = field.astype(right_ref.dtype)


def turn(right_ref, turned_ref):
    vectors = right_ref.shape[1] // 2
    for combo in range(right_ref.shape[0]):
        turned_ref[combo, :vectors] = -right_ref[combo, vectors:]
        turned_ref[combo, vectors:] = right_ref[combo, :vectors]


def row_block(combo, start, moves, here_ref, next_ref, shifts_ref, matrices_ref, right_ref, turned_ref, mid_ref, crossed_ref, out_ref):
    sites = here_ref.shape[-1]
    picks, count = out_ref.shape[1:3]
    direction = moves[combo, 1]
    rows = pl.ds(pl.multiple_of(start, TILE), count)
    block = plane_of(here_ref, next_ref, direction, (slice(None), slice(None), rows))
    half = COLORS * count
    both = jnp.dot(
        block.reshape(2 * half, sites), in_plane(shifts_ref, direction), preferred_element_type=jnp.float32
    )
    re, im = both[:half], both[half:]
    mid_ref[:half] = re
    mid_ref[half : 2 * half] = im - re
    mid_ref[2 * half :] = re + im
    result = None
    for column in range(COLORS):
        for lanes in range(sites // LANES):
            across = slice(lanes * LANES, (lanes + 1) * LANES)
            for tile in range(count // TILE):
                field = [
                    [
                        mid_ref[pl.ds(kind * half + row * count + tile * TILE, TILE), across]
                        for kind in range(3)
                    ]
                    for row in range(COLORS)
                ]
                for pick in range(picks):
                    sums = [None] * 3
                    for row in range(COLORS):
                        at = COLORS * (COLORS * column + row)
                        for kind in range(3):
                            entry = jnp.broadcast_to(
                                matrices_ref[combo, at + kind, pick : pick + 1, across], (TILE, LANES)
                            )
                            term = entry * field[row][kind]
                            sums[kind] = term if row == 0 else sums[kind] + term
                    down = slice(pick * count + tile * TILE, pick * count + (tile + 1) * TILE)
                    at = 2 * column * sites + lanes * LANES
                    crossed_ref[down, at : at + LANES] = (sums[0] - sums[2]).astype(jnp.bfloat16)
                    at += sites
                    crossed_ref[down, at : at + LANES] = (sums[0] + sums[1]).astype(jnp.bfloat16)
        deep = slice(2 * column * sites, 2 * (column + 1) * sites)
        wide = slice(column * sites, (column + 1) * sites)
        part = lax.dot_general(
            crossed_ref[:, deep],
            jnp.concatenate([right_ref[combo, :, wide], turned_ref[combo, :, wide]], axis=1),
            (((1,), (1,)), ((), ())),
            preferred_element_type=jnp.float32,
        )
        result = part if result is None else result + part
    out_ref[combo] = result.reshape(out_ref.shape[1:]).astype(out_ref.dtype)


def moves_of(meta, layout):
    ring, combos = layout

    class Moves:
        def __getitem__(self, key):
            combo, slot = key
            return meta[ring + 3 * combo + slot]

    class Rows:
        shape = (meta.shape[0] - ring - 3 * combos,)

        def __getitem__(self, i):
            return meta[ring + 3 * combos + i]

    return Moves(), Rows()


def prepare(of_next, layout, scale, meta, here_ref, next_ref, links_ref, shifts_ref, right_ref, matrices_ref):
    moves, rows = moves_of(meta, layout)
    for combo in range(layout[1]):

        @pl.when((moves[combo, 0] == 3) == of_next)
        def _(combo=combo):
            site_matrices(combo, moves, rows, here_ref, next_ref, links_ref, shifts_ref, matrices_ref, scale)

        @pl.when((moves[combo, 2] == 3) == of_next)
        def _(combo=combo):
            right_operand(combo, moves, here_ref, next_ref, shifts_ref, right_ref)


def early_kernel(layout, scale, meta, here_ref, links_ref, shifts_ref, right_ref, matrices_ref, copy_ref):
    copy_ref[...] = here_ref[...]
    prepare(False, layout, scale, meta, here_ref, here_ref, links_ref, shifts_ref, right_ref, matrices_ref)


def first_kernel(layout, scale, meta, here_ref, next_ref, links_ref, shifts_ref, right_in, matrices_in, right_ref, matrices_ref, out_ref, turned_ref, mid_ref, crossed_ref):
    prepare(True, layout, scale, meta, here_ref, next_ref, links_ref, shifts_ref, right_ref, matrices_ref)
    turn(right_ref, turned_ref)
    moves, _ = moves_of(meta, layout)
    for combo in range(layout[1]):
        row_block(combo, meta[0], moves, here_ref, next_ref, shifts_ref, matrices_ref, right_ref, turned_ref, mid_ref.at[combo], crossed_ref.at[combo], out_ref)


def block_kernel(number, layout, meta, here_ref, next_ref, shifts_ref, right_ref, matrices_ref, out_ref, turned_ref, mid_ref, crossed_ref):
    turn(right_ref, turned_ref)
    moves, _ = moves_of(meta, layout)
    for combo in range(layout[1]):
        row_block(combo, meta[number], moves, here_ref, next_ref, shifts_ref, matrices_ref, right_ref, turned_ref, mid_ref.at[combo], crossed_ref.at[combo], out_ref)


def local_work(eigenvectors, gauge_links, displacements, block_rows):
    parts, vectors, colors, planes, sites = eigenvectors.shape
    ring = lax.axis_size("site")
    me = lax.axis_index("site")
    combos, picks = displacements.shape[0], block_rows.shape[0]
    layout = (ring, combos)
    count = vectors // ring
    scale = 1.0 / math.sqrt(24.0 * planes * ring * sites)
    here = jnp.transpose(eigenvectors, (0, 2, 3, 1, 4)).reshape(parts, colors, vectors, sites)
    after = shifted(here, "site", -1)
    links = jnp.transpose(gauge_links, (1, 2, 3, 0, 4, 5)).astype(jnp.float32)
    links = links.reshape(COLORS, colors * colors * parts, sites)
    shifts = shift_matrices(sites, LX)
    last = ring - 1
    folded = ring == 4
    if folded:
        owners = [last - me, lax.rem(me + 2, ring), me + 1 - 2 * lax.rem(me, 2), me]
    else:
        owners = [lax.rem(me + offset, ring) for offset in range(1, ring + 1)]
    meta = jnp.concatenate(
        [jnp.stack(owners) * count, displacements.reshape(-1), block_rows]
    ).astype(jnp.int32)

    smem = pl.BlockSpec(memory_space=pltpu.SMEM)
    vmem = pl.BlockSpec(memory_space=pltpu.VMEM)
    right = jax.ShapeDtypeStruct((combos, parts * vectors, colors * sites), jnp.bfloat16)
    matrices = jax.ShapeDtypeStruct((combos, 3 * colors * colors, picks, sites), jnp.float32)
    scratch = [
        pltpu.VMEM(right.shape, right.dtype),
        pltpu.VMEM((combos, 3 * colors * count, sites), jnp.float32),
        pltpu.VMEM((combos, picks * count, parts * colors * sites), jnp.bfloat16),
    ]
    params = pltpu.CompilerParams(vmem_limit_bytes=VMEM_BYTES)

    def chunk(kind):
        return jax.ShapeDtypeStruct((combos, picks, count, 2 * vectors), kind)

    right, matrices, here = pl.pallas_call(
        functools.partial(early_kernel, layout, scale),
        out_shape=(right, matrices, jax.ShapeDtypeStruct(here.shape, here.dtype)),
        in_specs=[smem, vmem, vmem, vmem],
        out_specs=(vmem, vmem, vmem),
        compiler_params=params,
        cost_estimate=pl.CostEstimate(flops=500_000_000, bytes_accessed=4_000_000, transcendentals=0),
        name="early",
    )(meta, here, links, shifts)
    right, matrices, sent = pl.pallas_call(
        functools.partial(first_kernel, layout, scale),
        out_shape=(
            jax.ShapeDtypeStruct(right.shape, right.dtype),
            jax.ShapeDtypeStruct(matrices.shape, matrices.dtype),
            chunk(jnp.bfloat16),
        ),
        in_specs=[smem, vmem, vmem, vmem, vmem, vmem, vmem],
        out_specs=(vmem, vmem, vmem),
        input_output_aliases={5: 0, 6: 1},
        scratch_shapes=scratch,
        compiler_params=params,
        name="first",
    )(meta, here, after, links, shifts, right, matrices)
    blocks = [sent]
    for number in range(1, ring):
        blocks.append(
            pl.pallas_call(
                functools.partial(block_kernel, number, layout),
                out_shape=chunk(jnp.float32 if number == last else jnp.bfloat16),
                in_specs=[smem, vmem, vmem, vmem, vmem, vmem],
                out_specs=vmem,
                scratch_shapes=scratch,
                compiler_params=params,
                cost_estimate=pl.CostEstimate(flops=1_000_000_000, bytes_accessed=4_000_000, transcendentals=0),
            )(meta, here, after, shifts, right, matrices)
        )
    own = blocks.pop()
    if not folded:
        arrived = [shifted(block, "site", offset + 1) for offset, block in enumerate(blocks)]
        return functools.reduce(lambda total, block: total + block.astype(jnp.float32), arrived, own)
    near = lax.ppermute(blocks[0], "site", [(1, 2), (2, 1)])
    passed = lax.ppermute(blocks[0], "site", [(0, 1), (3, 2)])
    inward = lax.ppermute(blocks[1], "site", [(0, 2), (3, 1)])
    paired = lax.ppermute(blocks[2], "site", [(0, 1), (1, 0), (2, 3), (3, 2)])
    far = lax.ppermute(blocks[1] + passed, "site", [(1, 3), (2, 0)])
    held = own + near.astype(jnp.float32) + inward.astype(jnp.float32) + paired.astype(jnp.float32)
    held = lax.optimization_barrier(held)
    return held + far.astype(jnp.float32)


def solution(mesh):
    step = jax.shard_map(
        local_work,
        mesh=mesh,
        in_specs=(
            P("ta", None, None, "site", None),
            P("ta", None, None, None, "site", None),
            P(),
            P(),
        ),
        out_specs=P("ta", None, "site", None),
        check_vma=False,
    )
    if mesh.shape["site"] != 4:
        return step
    return step
```

```python
import functools
import math

import jax
import jax.numpy as jnp
from jax import lax
from jax.experimental import pallas as pl
from jax.experimental.pallas import tpu as pltpu
from jax.sharding import PartitionSpec as P


LX = 16
COLORS = 3
TILE = 16
LANES = 128
SUBLANES = 8
VMEM_BYTES = 16 * 2**20


def shifted(block, axis, distance):
    count = lax.axis_size(axis)
    return lax.ppermute(block, axis, [(i, (i + distance) % count) for i in range(count)])


def shift_matrices(sites, width_x):
    source = lax.broadcasted_iota(jnp.int32, (COLORS, sites, sites), 1)
    target = lax.broadcasted_iota(jnp.int32, (COLORS, sites, sites), 2)
    direction = lax.broadcasted_iota(jnp.int32, (COLORS, sites, sites), 0)
    column = lax.rem(target, width_x)
    along_x = target - column + lax.rem(column + 1, width_x)
    along_y = lax.rem(target + width_x, sites)
    neighbour = jnp.where(direction == 1, along_x, jnp.where(direction == 2, along_y, target))
    return jnp.where(source == neighbour, 1.0, 0.0).astype(jnp.bfloat16)


def in_plane(shifts_ref, direction):
    return shifts_ref[jnp.where(direction == 3, 0, direction)]


def mul(left, right):
    return left[0] * right[0] - left[1] * right[1], left[0] * right[1] + left[1] * right[0]


def add(left, right):
    return left[0] + right[0], left[1] + right[1]


def plane_of(here_ref, next_ref, direction, index):
    return jnp.where(direction == 3, next_ref[index], here_ref[index])


def chosen_link(links_ref, direction):
    which = jnp.maximum(direction - 1, 0)
    resting = direction == 0

    def entry(row, column):
        at = 2 * (COLORS * row + column)
        re = links_ref[which, at : at + 1, :]
        im = links_ref[which, at + 1 : at + 2, :]
        unit = jnp.full_like(re, 1.0 if row == column else 0.0)
        return jnp.where(resting, unit, re), jnp.where(resting, jnp.zeros_like(im), im)

    return [[entry(row, column) for column in range(COLORS)] for row in range(COLORS)]


def site_matrices(combo, moves, rows, here_ref, next_ref, links_ref, shifts_ref, matrices_ref, scale):
    vectors = here_ref.shape[-2]
    direction = moves[combo, 0]
    kept, picks = matrices_ref.shape[2], SUBLANES
    numbers = lax.broadcasted_iota(jnp.int32, (picks, vectors), 1)
    lane = lax.broadcasted_iota(jnp.int32, (picks, vectors), 0)
    wanted = jnp.full((picks, vectors), -1, jnp.int32)
    for i in range(rows.shape[0]):
        wanted = jnp.where(lane == i, rows[i], wanted)
    select = jnp.where(numbers == wanted, 1.0, 0.0).astype(jnp.bfloat16)

    def picked(part, color):
        return jnp.dot(
            select,
            plane_of(here_ref, next_ref, direction, (part, color)),
            preferred_element_type=jnp.float32,
        )

    stacked = jnp.concatenate(
        [picked(part, color) for color in range(COLORS) for part in range(2)], axis=0
    )
    stacked = jnp.dot(
        stacked.astype(jnp.bfloat16), in_plane(shifts_ref, direction), preferred_element_type=jnp.float32
    )
    fields = [
        tuple(stacked[at * picks : (at + 1) * picks] for at in (2 * color, 2 * color + 1))
        for color in range(COLORS)
    ]
    first, second, third = (chosen_link(links_ref, moves[combo, slot]) for slot in range(3))

    def total(terms):
        return functools.reduce(add, terms)

    left = [
        total(mul(first[a][b], fields[b]) for b in range(COLORS)) for a in range(COLORS)
    ]
    left = [(re * scale, im * scale) for re, im in left]
    for column in range(COLORS):
        after = []
        for b in range(COLORS):
            up, down = (b + 1) % COLORS, (b + 2) % COLORS
            plus = mul(third[up][column], left[down])
            minus = mul(third[down][column], left[up])
            after.append((plus[0] - minus[0], plus[1] - minus[1]))
        for row in range(COLORS):
            re, im = total(mul(second[b][row], after[b]) for b in range(COLORS))
            at = COLORS * (COLORS * column + row)
            matrices_ref[combo, at] = (re + im)[:kept]
            matrices_ref[combo, at + 1] = re[:kept]
            matrices_ref[combo, at + 2] = im[:kept]


def right_operand(combo, moves, here_ref, next_ref, shifts_ref, right_ref):
    vectors, sites = here_ref.shape[-2:]
    direction = moves[combo, 2]
    shift = in_plane(shifts_ref, direction)
    for color in range(COLORS):
        for part in range(2):
            field = jnp.dot(
                plane_of(here_ref, next_ref, direction, (part, color)),
                shift,
                preferred_element_type=jnp.float32,
            )
            right_ref[
                combo, part * vectors : (part + 1) * vectors, color * sites : (color + 1) * sites
            ] = field.astype(right_ref.dtype)


def turn(right_ref, turned_ref):
    vectors = right_ref.shape[1] // 2
    for combo in range(right_ref.shape[0]):
        turned_ref[combo, :vectors] = -right_ref[combo, vectors:]
        turned_ref[combo, vectors:] = right_ref[combo, :vectors]


def row_block(combo, start, moves, here_ref, next_ref, shifts_ref, matrices_ref, right_ref, turned_ref, mid_ref, crossed_ref, out_ref):
    sites = here_ref.shape[-1]
    picks, count = out_ref.shape[1:3]
    direction = moves[combo, 1]
    rows = pl.ds(pl.multiple_of(start, TILE), count)
    block = plane_of(here_ref, next_ref, direction, (slice(None), slice(None), rows))
    half = COLORS * count
    both = jnp.dot(
        block.reshape(2 * half, sites), in_plane(shifts_ref, direction), preferred_element_type=jnp.float32
    )
    re, im = both[:half], both[half:]
    mid_ref[:half] = re
    mid_ref[half : 2 * half] = im - re
    mid_ref[2 * half :] = re + im
    result = None
    for column in range(COLORS):
        for lanes in range(sites // LANES):
            across = slice(lanes * LANES, (lanes + 1) * LANES)
            for tile in range(count // TILE):
                field = [
                    [
                        mid_ref[pl.ds(kind * half + row * count + tile * TILE, TILE), across]
                        for kind in range(3)
                    ]
                    for row in range(COLORS)
                ]
                for pick in range(picks):
                    sums = [None] * 3
                    for row in range(COLORS):
                        at = COLORS * (COLORS * column + row)
                        for kind in range(3):
                            entry = jnp.broadcast_to(
                                matrices_ref[combo, at + kind, pick : pick + 1, across], (TILE, LANES)
                            )
                            term = entry * field[row][kind]
                            sums[kind] = term if row == 0 else sums[kind] + term
                    down = slice(pick * count + tile * TILE, pick * count + (tile + 1) * TILE)
                    at = 2 * column * sites + lanes * LANES
                    crossed_ref[down, at : at + LANES] = (sums[0] - sums[2]).astype(jnp.bfloat16)
                    at += sites
                    crossed_ref[down, at : at + LANES] = (sums[0] + sums[1]).astype(jnp.bfloat16)
        deep = slice(2 * column * sites, 2 * (column + 1) * sites)
        wide = slice(column * sites, (column + 1) * sites)
        part = lax.dot_general(
            crossed_ref[:, deep],
            jnp.concatenate([right_ref[combo, :, wide], turned_ref[combo, :, wide]], axis=1),
            (((1,), (1,)), ((), ())),
            preferred_element_type=jnp.float32,
        )
        result = part if result is None else result + part
    out_ref[combo] = result.reshape(out_ref.shape[1:]).astype(out_ref.dtype)


def moves_of(meta, layout):
    ring, combos = layout

    class Moves:
        def __getitem__(self, key):
            combo, slot = key
            return meta[ring + 3 * combo + slot]

    class Rows:
        shape = (meta.shape[0] - ring - 3 * combos,)

        def __getitem__(self, i):
            return meta[ring + 3 * combos + i]

    return Moves(), Rows()


def prepare(of_next, layout, scale, meta, here_ref, next_ref, links_ref, shifts_ref, right_ref, matrices_ref):
    moves, rows = moves_of(meta, layout)
    for combo in range(layout[1]):

        @pl.when((moves[combo, 0] == 3) == of_next)
        def _(combo=combo):
            site_matrices(combo, moves, rows, here_ref, next_ref, links_ref, shifts_ref, matrices_ref, scale)

        @pl.when((moves[combo, 2] == 3) == of_next)
        def _(combo=combo):
            right_operand(combo, moves, here_ref, next_ref, shifts_ref, right_ref)


def early_kernel(layout, scale, meta, here_ref, links_ref, shifts_ref, right_ref, matrices_ref, copy_ref):
    copy_ref[...] = here_ref[...]
    prepare(False, layout, scale, meta, here_ref, here_ref, links_ref, shifts_ref, right_ref, matrices_ref)


def first_kernel(layout, scale, meta, here_ref, next_ref, links_ref, shifts_ref, right_in, matrices_in, right_ref, matrices_ref, out_ref, turned_ref, mid_ref, crossed_ref):
    prepare(True, layout, scale, meta, here_ref, next_ref, links_ref, shifts_ref, right_ref, matrices_ref)
    turn(right_ref, turned_ref)
    moves, _ = moves_of(meta, layout)
    for combo in range(layout[1]):
        row_block(combo, meta[0], moves, here_ref, next_ref, shifts_ref, matrices_ref, right_ref, turned_ref, mid_ref.at[combo], crossed_ref.at[combo], out_ref)


def block_kernel(number, layout, meta, here_ref, next_ref, shifts_ref, right_ref, matrices_ref, out_ref, turned_ref, mid_ref, crossed_ref):
    turn(right_ref, turned_ref)
    moves, _ = moves_of(meta, layout)
    for combo in range(layout[1]):
        row_block(combo, meta[number], moves, here_ref, next_ref, shifts_ref, matrices_ref, right_ref, turned_ref, mid_ref.at[combo], crossed_ref.at[combo], out_ref)


def local_work(eigenvectors, gauge_links, displacements, block_rows):
    parts, vectors, colors, planes, sites = eigenvectors.shape
    ring = lax.axis_size("site")
    me = lax.axis_index("site")
    combos, picks = displacements.shape[0], block_rows.shape[0]
    layout = (ring, combos)
    count = vectors // ring
    scale = 1.0 / math.sqrt(24.0 * planes * ring * sites)
    here = jnp.transpose(eigenvectors, (0, 2, 3, 1, 4)).reshape(parts, colors, vectors, sites)
    after = shifted(here, "site", -1)
    links = jnp.transpose(gauge_links, (1, 2, 3, 0, 4, 5)).astype(jnp.float32)
    links = links.reshape(COLORS, colors * colors * parts, sites)
    shifts = shift_matrices(sites, LX)
    last = ring - 1
    folded = ring == 4
    if folded:
        owners = [last - me, lax.rem(me + 2, ring), me + 1 - 2 * lax.rem(me, 2), me]
    else:
        owners = [lax.rem(me + offset, ring) for offset in range(1, ring + 1)]
    meta = jnp.concatenate(
        [jnp.stack(owners) * count, displacements.reshape(-1), block_rows]
    ).astype(jnp.int32)

    smem = pl.BlockSpec(memory_space=pltpu.SMEM)
    vmem = pl.BlockSpec(memory_space=pltpu.VMEM)
    right = jax.ShapeDtypeStruct((combos, parts * vectors, colors * sites), jnp.bfloat16)
    matrices = jax.ShapeDtypeStruct((combos, 3 * colors * colors, picks, sites), jnp.float32)
    scratch = [
        pltpu.VMEM(right.shape, right.dtype),
        pltpu.VMEM((combos, 3 * colors * count, sites), jnp.float32),
        pltpu.VMEM((combos, picks * count, parts * colors * sites), jnp.bfloat16),
    ]
    params = pltpu.CompilerParams(vmem_limit_bytes=VMEM_BYTES)

    def chunk(kind):
        return jax.ShapeDtypeStruct((combos, picks, count, 2 * vectors), kind)

    right, matrices, here = pl.pallas_call(
        functools.partial(early_kernel, layout, scale),
        out_shape=(right, matrices, jax.ShapeDtypeStruct(here.shape, here.dtype)),
        in_specs=[smem, vmem, vmem, vmem],
        out_specs=(vmem, vmem, vmem),
        compiler_params=params,
        cost_estimate=pl.CostEstimate(flops=500_000_000, bytes_accessed=4_000_000, transcendentals=0),
        name="early",
    )(meta, here, links, shifts)
    right, matrices, sent = pl.pallas_call(
        functools.partial(first_kernel, layout, scale),
        out_shape=(
            jax.ShapeDtypeStruct(right.shape, right.dtype),
            jax.ShapeDtypeStruct(matrices.shape, matrices.dtype),
            chunk(jnp.bfloat16),
        ),
        in_specs=[smem, vmem, vmem, vmem, vmem, vmem, vmem],
        out_specs=(vmem, vmem, vmem),
        input_output_aliases={5: 0, 6: 1},
        scratch_shapes=scratch,
        compiler_params=params,
        name="first",
    )(meta, here, after, links, shifts, right, matrices)
    blocks = [sent]
    for number in range(1, ring):
        blocks.append(
            pl.pallas_call(
                functools.partial(block_kernel, number, layout),
                out_shape=chunk(jnp.float32 if number == last else jnp.bfloat16),
                in_specs=[smem, vmem, vmem, vmem, vmem, vmem],
                out_specs=vmem,
                scratch_shapes=scratch,
                compiler_params=params,
                cost_estimate=pl.CostEstimate(flops=1_000_000_000, bytes_accessed=4_000_000, transcendentals=0),
            )(meta, here, after, shifts, right, matrices)
        )
    own = blocks.pop()
    if not folded:
        arrived = [shifted(block, "site", offset + 1) for offset, block in enumerate(blocks)]
        return functools.reduce(lambda total, block: total + block.astype(jnp.float32), arrived, own)
    mirrored = lax.ppermute(blocks[0], "site", [(i, last - i) for i in range(ring)])
    far = shifted(blocks[1], "site", 2)
    paired = lax.ppermute(blocks[2], "site", [(0, 1), (1, 0), (2, 3), (3, 2)])
    held = own + mirrored.astype(jnp.float32) + paired.astype(jnp.float32)
    held = lax.optimization_barrier(held)
    return held + far.astype(jnp.float32)


def solution(mesh):
    step = jax.shard_map(
        local_work,
        mesh=mesh,
        in_specs=(
            P("ta", None, None, "site", None),
            P("ta", None, None, None, "site", None),
            P(),
            P(),
        ),
        out_specs=P("ta", None, "site", None),
        check_vma=False,
    )
    if mesh.shape["site"] != 4:
        return step
    return step
```

```python
import functools
import math

import jax
import jax.numpy as jnp
from jax import lax
from jax.experimental import pallas as pl
from jax.experimental.pallas import tpu as pltpu
from jax.sharding import PartitionSpec as P


LX = 16
COLORS = 3
TILE = 16
LANES = 128
SUBLANES = 8
VMEM_BYTES = 16 * 2**20


def shifted(block, axis, distance):
    count = lax.axis_size(axis)
    return lax.ppermute(block, axis, [(i, (i + distance) % count) for i in range(count)])


def shift_matrices(sites, width_x):
    source = lax.broadcasted_iota(jnp.int32, (COLORS, sites, sites), 1)
    target = lax.broadcasted_iota(jnp.int32, (COLORS, sites, sites), 2)
    direction = lax.broadcasted_iota(jnp.int32, (COLORS, sites, sites), 0)
    column = lax.rem(target, width_x)
    along_x = target - column + lax.rem(column + 1, width_x)
    along_y = lax.rem(target + width_x, sites)
    neighbour = jnp.where(direction == 1, along_x, jnp.where(direction == 2, along_y, target))
    return jnp.where(source == neighbour, 1.0, 0.0).astype(jnp.bfloat16)


def in_plane(shifts_ref, direction):
    return shifts_ref[jnp.where(direction == 3, 0, direction)]


def mul(left, right):
    return left[0] * right[0] - left[1] * right[1], left[0] * right[1] + left[1] * right[0]


def add(left, right):
    return left[0] + right[0], left[1] + right[1]


def plane_of(here_ref, next_ref, direction, index):
    return jnp.where(direction == 3, next_ref[index], here_ref[index])


def chosen_link(links_ref, direction):
    which = jnp.maximum(direction - 1, 0)
    resting = direction == 0

    def entry(row, column):
        at = 2 * (COLORS * row + column)
        re = links_ref[which, at : at + 1, :]
        im = links_ref[which, at + 1 : at + 2, :]
        unit = jnp.full_like(re, 1.0 if row == column else 0.0)
        return jnp.where(resting, unit, re), jnp.where(resting, jnp.zeros_like(im), im)

    return [[entry(row, column) for column in range(COLORS)] for row in range(COLORS)]


def join_links(combo, moves, links_ref, joins_ref, scale):
    first, second, third = (chosen_link(links_ref, moves[combo, slot]) for slot in range(3))
    for a in range(COLORS):
        for b in range(COLORS):
            for part in range(2):
                at = 2 * (COLORS * a + b) + part
                joins_ref[combo, at : at + 1, :] = first[a][b][part] * scale
    for a in range(COLORS):
        up, down = (a + 1) % COLORS, (a + 2) % COLORS
        for column in range(COLORS):
            for row in range(COLORS):
                plus = mul(second[up][row], third[down][column])
                minus = mul(second[down][row], third[up][column])
                at = 2 * (COLORS * COLORS * (1 + a) + COLORS * column + row)
                for part in range(2):
                    joins_ref[combo, at + part : at + part + 1, :] = plus[part] - minus[part]


def site_matrices(combo, rows, plane_ref, shift, joins_ref, matrices_ref):
    vectors = plane_ref.shape[-2]
    kept, picks = matrices_ref.shape[2], SUBLANES
    numbers = lax.broadcasted_iota(jnp.int32, (picks, vectors), 1)
    lane = lax.broadcasted_iota(jnp.int32, (picks, vectors), 0)
    wanted = jnp.full((picks, vectors), -1, jnp.int32)
    for i in range(rows.shape[0]):
        wanted = jnp.where(lane == i, rows[i], wanted)
    select = jnp.where(numbers == wanted, 1.0, 0.0).astype(jnp.bfloat16)
    stacked = jnp.concatenate(
        [
            jnp.dot(select, plane_ref[part, color], preferred_element_type=jnp.float32)
            for color in range(COLORS)
            for part in range(2)
        ],
        axis=0,
    )
    if shift is not None:
        stacked = jnp.dot(stacked.astype(jnp.bfloat16), shift, preferred_element_type=jnp.float32)
    fields = [
        tuple(stacked[at * picks : (at + 1) * picks] for at in (2 * color, 2 * color + 1))
        for color in range(COLORS)
    ]

    def joined(at):
        return tuple(joins_ref[combo, 2 * at + part : 2 * at + part + 1, :] for part in range(2))

    def total(terms):
        return functools.reduce(add, terms)

    left = [
        total(mul(joined(COLORS * a + b), fields[b]) for b in range(COLORS)) for a in range(COLORS)
    ]
    for place in range(COLORS * COLORS):
        re, im = total(
            mul(joined(COLORS * COLORS * (1 + a) + place), left[a]) for a in range(COLORS)
        )
        at = COLORS * place
        matrices_ref[combo, at] = (re + im)[:kept]
        matrices_ref[combo, at + 1] = re[:kept]
        matrices_ref[combo, at + 2] = im[:kept]


def right_operand(combo, plane_ref, shift, right_ref):
    vectors, sites = plane_ref.shape[-2:]
    for color in range(COLORS):
        for part in range(2):
            field = plane_ref[part, color]
            if shift is not None:
                field = jnp.dot(field, shift, preferred_element_type=jnp.float32)
            right_ref[
                combo, part * vectors : (part + 1) * vectors, color * sites : (color + 1) * sites
            ] = field.astype(right_ref.dtype)


def turn(right_ref, turned_ref):
    vectors = right_ref.shape[1] // 2
    for combo in range(right_ref.shape[0]):
        turned_ref[combo, :vectors] = -right_ref[combo, vectors:]
        turned_ref[combo, vectors:] = right_ref[combo, :vectors]


def row_block(combo, start, moves, here_ref, next_ref, shifts_ref, matrices_ref, right_ref, turned_ref, mid_ref, crossed_ref, out_ref):
    sites = here_ref.shape[-1]
    picks, count = out_ref.shape[1:3]
    direction = moves[combo, 1]
    rows = pl.ds(pl.multiple_of(start, TILE), count)
    block = plane_of(here_ref, next_ref, direction, (slice(None), slice(None), rows))
    half = COLORS * count
    both = jnp.dot(
        block.reshape(2 * half, sites), in_plane(shifts_ref, direction), preferred_element_type=jnp.float32
    )
    re, im = both[:half], both[half:]
    mid_ref[:half] = re
    mid_ref[half : 2 * half] = im - re
    mid_ref[2 * half :] = re + im
    result = None
    for column in range(COLORS):
        for lanes in range(sites // LANES):
            across = slice(lanes * LANES, (lanes + 1) * LANES)
            for tile in range(count // TILE):
                field = [
                    [
                        mid_ref[pl.ds(kind * half + row * count + tile * TILE, TILE), across]
                        for kind in range(3)
                    ]
                    for row in range(COLORS)
                ]
                for pick in range(picks):
                    sums = [None] * 3
                    for row in range(COLORS):
                        at = COLORS * (COLORS * column + row)
                        for kind in range(3):
                            entry = jnp.broadcast_to(
                                matrices_ref[combo, at + kind, pick : pick + 1, across], (TILE, LANES)
                            )
                            term = entry * field[row][kind]
                            sums[kind] = term if row == 0 else sums[kind] + term
                    down = slice(pick * count + tile * TILE, pick * count + (tile + 1) * TILE)
                    at = 2 * column * sites + lanes * LANES
                    crossed_ref[down, at : at + LANES] = (sums[0] - sums[2]).astype(jnp.bfloat16)
                    at += sites
                    crossed_ref[down, at : at + LANES] = (sums[0] + sums[1]).astype(jnp.bfloat16)
        deep = slice(2 * column * sites, 2 * (column + 1) * sites)
        wide = slice(column * sites, (column + 1) * sites)
        part = lax.dot_general(
            crossed_ref[:, deep],
            jnp.concatenate([right_ref[combo, :, wide], turned_ref[combo, :, wide]], axis=1),
            (((1,), (1,)), ((), ())),
            preferred_element_type=jnp.float32,
        )
        result = part if result is None else result + part
    out_ref[combo] = result.reshape(out_ref.shape[1:]).astype(out_ref.dtype)


def moves_of(meta, layout):
    ring, combos = layout

    class Moves:
        def __getitem__(self, key):
            combo, slot = key
            return meta[ring + 3 * combo + slot]

    class Rows:
        shape = (meta.shape[0] - ring - 3 * combos,)

        def __getitem__(self, i):
            return meta[ring + 3 * combos + i]

    return Moves(), Rows()


def prepare(of_next, layout, meta, plane_ref, shifts_ref, joins_ref, right_ref, matrices_ref):
    moves, rows = moves_of(meta, layout)
    for combo in range(layout[1]):

        @pl.when((moves[combo, 0] == 3) == of_next)
        def _(combo=combo):
            shift = None if of_next else in_plane(shifts_ref, moves[combo, 0])
            site_matrices(combo, rows, plane_ref, shift, joins_ref, matrices_ref)

        @pl.when((moves[combo, 2] == 3) == of_next)
        def _(combo=combo):
            shift = None if of_next else in_plane(shifts_ref, moves[combo, 2])
            right_operand(combo, plane_ref, shift, right_ref)


def early_kernel(layout, scale, meta, here_ref, links_ref, shifts_ref, right_ref, matrices_ref, copy_ref, joins_ref):
    copy_ref[...] = here_ref[...]
    moves, _ = moves_of(meta, layout)
    for combo in range(layout[1]):
        join_links(combo, moves, links_ref, joins_ref, scale)
    prepare(False, layout, meta, here_ref, shifts_ref, joins_ref, right_ref, matrices_ref)


def first_kernel(layout, meta, here_ref, next_ref, joins_ref, shifts_ref, right_in, matrices_in, right_ref, matrices_ref, out_ref, turned_ref, mid_ref, crossed_ref):
    prepare(True, layout, meta, next_ref, shifts_ref, joins_ref, right_ref, matrices_ref)
    turn(right_ref, turned_ref)
    moves, _ = moves_of(meta, layout)
    for combo in range(layout[1]):
        row_block(combo, meta[0], moves, here_ref, next_ref, shifts_ref, matrices_ref, right_ref, turned_ref, mid_ref.at[combo], crossed_ref.at[combo], out_ref)


def block_kernel(number, layout, meta, here_ref, next_ref, shifts_ref, right_ref, matrices_ref, out_ref, turned_ref, mid_ref, crossed_ref):
    turn(right_ref, turned_ref)
    moves, _ = moves_of(meta, layout)
    for combo in range(layout[1]):
        row_block(combo, meta[number], moves, here_ref, next_ref, shifts_ref, matrices_ref, right_ref, turned_ref, mid_ref.at[combo], crossed_ref.at[combo], out_ref)


def local_work(eigenvectors, gauge_links, displacements, block_rows):
    parts, vectors, colors, planes, sites = eigenvectors.shape
    ring = lax.axis_size("site")
    me = lax.axis_index("site")
    combos, picks = displacements.shape[0], block_rows.shape[0]
    layout = (ring, combos)
    count = vectors // ring
    scale = 1.0 / math.sqrt(24.0 * planes * ring * sites)
    here = jnp.transpose(eigenvectors, (0, 2, 3, 1, 4)).reshape(parts, colors, vectors, sites)
    after = shifted(here, "site", -1)
    links = jnp.transpose(gauge_links, (1, 2, 3, 0, 4, 5)).astype(jnp.float32)
    links = links.reshape(COLORS, colors * colors * parts, sites)
    shifts = shift_matrices(sites, LX)
    last = ring - 1
    folded = ring == 4
    if folded:
        owners = [last - me, lax.rem(me + 2, ring), me + 1 - 2 * lax.rem(me, 2), me]
    else:
        owners = [lax.rem(me + offset, ring) for offset in range(1, ring + 1)]
    meta = jnp.concatenate(
        [jnp.stack(owners) * count, displacements.reshape(-1), block_rows]
    ).astype(jnp.int32)

    smem = pl.BlockSpec(memory_space=pltpu.SMEM)
    vmem = pl.BlockSpec(memory_space=pltpu.VMEM)
    right = jax.ShapeDtypeStruct((combos, parts * vectors, colors * sites), jnp.bfloat16)
    matrices = jax.ShapeDtypeStruct((combos, 3 * colors * colors, picks, sites), jnp.float32)
    joins = jax.ShapeDtypeStruct((combos, 2 * (1 + colors) * colors * colors, sites), jnp.float32)
    scratch = [
        pltpu.VMEM(right.shape, right.dtype),
        pltpu.VMEM((combos, 3 * colors * count, sites), jnp.float32),
        pltpu.VMEM((combos, picks * count, parts * colors * sites), jnp.bfloat16),
    ]
    params = pltpu.CompilerParams(vmem_limit_bytes=VMEM_BYTES)

    def chunk(kind):
        return jax.ShapeDtypeStruct((combos, picks, count, 2 * vectors), kind)

    right, matrices, here, joins = pl.pallas_call(
        functools.partial(early_kernel, layout, scale),
        out_shape=(right, matrices, jax.ShapeDtypeStruct(here.shape, here.dtype), joins),
        in_specs=[smem, vmem, vmem, vmem],
        out_specs=(vmem, vmem, vmem, vmem),
        compiler_params=params,
        cost_estimate=pl.CostEstimate(flops=500_000_000, bytes_accessed=4_000_000, transcendentals=0),
        name="early",
    )(meta, here, links, shifts)
    right, matrices, sent = pl.pallas_call(
        functools.partial(first_kernel, layout),
        out_shape=(
            jax.ShapeDtypeStruct(right.shape, right.dtype),
            jax.ShapeDtypeStruct(matrices.shape, matrices.dtype),
            chunk(jnp.bfloat16),
        ),
        in_specs=[smem, vmem, vmem, vmem, vmem, vmem, vmem],
        out_specs=(vmem, vmem, vmem),
        input_output_aliases={5: 0, 6: 1},
        scratch_shapes=scratch,
        compiler_params=params,
        name="first",
    )(meta, here, after, joins, shifts, right, matrices)
    blocks = [sent]
    for number in range(1, ring):
        blocks.append(
            pl.pallas_call(
                functools.partial(block_kernel, number, layout),
                out_shape=chunk(jnp.float32 if number == last else jnp.bfloat16),
                in_specs=[smem, vmem, vmem, vmem, vmem, vmem],
                out_specs=vmem,
                scratch_shapes=scratch,
                compiler_params=params,
                cost_estimate=pl.CostEstimate(flops=1_000_000_000, bytes_accessed=4_000_000, transcendentals=0),
            )(meta, here, after, shifts, right, matrices)
        )
    own = blocks.pop()
    if not folded:
        arrived = [shifted(block, "site", offset + 1) for offset, block in enumerate(blocks)]
        return functools.reduce(lambda total, block: total + block.astype(jnp.float32), arrived, own)
    near = lax.ppermute(blocks[0], "site", [(1, 2), (2, 1)])
    passed = lax.ppermute(blocks[0], "site", [(0, 1), (3, 2)])
    far = shifted(blocks[1] + passed, "site", 2)
    paired = lax.ppermute(blocks[2], "site", [(0, 1), (1, 0), (2, 3), (3, 2)])
    held = own + near.astype(jnp.float32) + paired.astype(jnp.float32)
    held = lax.optimization_barrier(held)
    return held + far.astype(jnp.float32)


def solution(mesh):
    step = jax.shard_map(
        local_work,
        mesh=mesh,
        in_specs=(
            P("ta", None, None, "site", None),
            P("ta", None, None, None, "site", None),
            P(),
            P(),
        ),
        out_specs=P("ta", None, "site", None),
        check_vma=False,
    )
    if mesh.shape["site"] != 4:
        return step
    return step
```

```python
import functools
import math

import jax
import jax.numpy as jnp
from jax import lax
from jax.experimental import pallas as pl
from jax.experimental.pallas import tpu as pltpu
from jax.sharding import PartitionSpec as P


LX = 16
COLORS = 3
TILE = 16
LANES = 128
SUBLANES = 8
VMEM_BYTES = 16 * 2**20


def shifted(block, axis, distance):
    count = lax.axis_size(axis)
    return lax.ppermute(block, axis, [(i, (i + distance) % count) for i in range(count)])


def shift_matrices(sites, width_x):
    source = lax.broadcasted_iota(jnp.int32, (COLORS, sites, sites), 1)
    target = lax.broadcasted_iota(jnp.int32, (COLORS, sites, sites), 2)
    direction = lax.broadcasted_iota(jnp.int32, (COLORS, sites, sites), 0)
    column = lax.rem(target, width_x)
    along_x = target - column + lax.rem(column + 1, width_x)
    along_y = lax.rem(target + width_x, sites)
    neighbour = jnp.where(direction == 1, along_x, jnp.where(direction == 2, along_y, target))
    return jnp.where(source == neighbour, 1.0, 0.0).astype(jnp.bfloat16)


def in_plane(shifts_ref, direction):
    return shifts_ref[jnp.where(direction == 3, 0, direction)]


def middle_exchange(block):
    lines, ring = lax.axis_size("ta"), lax.axis_size("site")
    route = []
    for line in range(lines):
        beside = line ^ 1 if lines % 2 == 0 else line
        for site in range(ring):
            inner = 0 < site < ring - 1
            target = line * ring + ring - 1 - site if inner else beside * ring + site
            route.append((line * ring + site, target))
    return lax.ppermute(block, ("ta", "site"), route)


def mul(left, right):
    return left[0] * right[0] - left[1] * right[1], left[0] * right[1] + left[1] * right[0]


def add(left, right):
    return left[0] + right[0], left[1] + right[1]


def plane_of(here_ref, next_ref, direction, index):
    return jnp.where(direction == 3, next_ref[index], here_ref[index])


def chosen_link(links_ref, direction):
    which = jnp.maximum(direction - 1, 0)
    resting = direction == 0

    def entry(row, column):
        at = 2 * (COLORS * row + column)
        re = links_ref[which, at : at + 1, :]
        im = links_ref[which, at + 1 : at + 2, :]
        unit = jnp.full_like(re, 1.0 if row == column else 0.0)
        return jnp.where(resting, unit, re), jnp.where(resting, jnp.zeros_like(im), im)

    return [[entry(row, column) for column in range(COLORS)] for row in range(COLORS)]


def join_links(combo, moves, links_ref, joins_ref, scale):
    first, second, third = (chosen_link(links_ref, moves[combo, slot]) for slot in range(3))
    for a in range(COLORS):
        for b in range(COLORS):
            for part in range(2):
                at = 2 * (COLORS * a + b) + part
                joins_ref[combo, at : at + 1, :] = first[a][b][part] * scale
    for a in range(COLORS):
        up, down = (a + 1) % COLORS, (a + 2) % COLORS
        for column in range(COLORS):
            for row in range(COLORS):
                plus = mul(second[up][row], third[down][column])
                minus = mul(second[down][row], third[up][column])
                at = 2 * (COLORS * COLORS * (1 + a) + COLORS * column + row)
                for part in range(2):
                    joins_ref[combo, at + part : at + part + 1, :] = plus[part] - minus[part]


def site_matrices(combo, rows, plane_ref, shift, joins_ref, matrices_ref):
    vectors = plane_ref.shape[-2]
    kept, picks = matrices_ref.shape[2], SUBLANES
    numbers = lax.broadcasted_iota(jnp.int32, (picks, vectors), 1)
    lane = lax.broadcasted_iota(jnp.int32, (picks, vectors), 0)
    wanted = jnp.full((picks, vectors), -1, jnp.int32)
    for i in range(rows.shape[0]):
        wanted = jnp.where(lane == i, rows[i], wanted)
    select = jnp.where(numbers == wanted, 1.0, 0.0).astype(jnp.bfloat16)
    stacked = jnp.concatenate(
        [
            jnp.dot(select, plane_ref[part, color], preferred_element_type=jnp.float32)
            for color in range(COLORS)
            for part in range(2)
        ],
        axis=0,
    )
    if shift is not None:
        stacked = jnp.dot(stacked.astype(jnp.bfloat16), shift, preferred_element_type=jnp.float32)
    fields = [
        tuple(stacked[at * picks : (at + 1) * picks] for at in (2 * color, 2 * color + 1))
        for color in range(COLORS)
    ]

    def joined(at):
        return tuple(joins_ref[combo, 2 * at + part : 2 * at + part + 1, :] for part in range(2))

    def total(terms):
        return functools.reduce(add, terms)

    left = [
        total(mul(joined(COLORS * a + b), fields[b]) for b in range(COLORS)) for a in range(COLORS)
    ]
    for place in range(COLORS * COLORS):
        re, im = total(
            mul(joined(COLORS * COLORS * (1 + a) + place), left[a]) for a in range(COLORS)
        )
        at = COLORS * place
        matrices_ref[combo, at] = (re + im)[:kept]
        matrices_ref[combo, at + 1] = re[:kept]
        matrices_ref[combo, at + 2] = im[:kept]


def right_operand(combo, plane_ref, shift, right_ref):
    vectors, sites = plane_ref.shape[-2:]
    for color in range(COLORS):
        for part in range(2):
            field = jnp.dot(plane_ref[part, color], shift, preferred_element_type=jnp.float32)
            right_ref[
                combo, part * vectors : (part + 1) * vectors, color * sites : (color + 1) * sites
            ] = field.astype(right_ref.dtype)


def turn(right_ref, turned_ref):
    vectors = right_ref.shape[1] // 2
    for combo in range(right_ref.shape[0]):
        turned_ref[combo, :vectors] = -right_ref[combo, vectors:]
        turned_ref[combo, vectors:] = right_ref[combo, :vectors]


def row_block(combo, start, moves, here_ref, next_ref, shifts_ref, matrices_ref, right_ref, turned_ref, mid_ref, crossed_ref, out_ref):
    sites = here_ref.shape[-1]
    picks, count = out_ref.shape[1:3]
    direction = moves[combo, 1]
    rows = pl.ds(pl.multiple_of(start, TILE), count)
    block = plane_of(here_ref, next_ref, direction, (slice(None), slice(None), rows))
    half = COLORS * count
    both = jnp.dot(
        block.reshape(2 * half, sites), in_plane(shifts_ref, direction), preferred_element_type=jnp.float32
    )
    re, im = both[:half], both[half:]
    mid_ref[:half] = re
    mid_ref[half : 2 * half] = im - re
    mid_ref[2 * half :] = re + im
    result = None
    for column in range(COLORS):
        for lanes in range(sites // LANES):
            across = slice(lanes * LANES, (lanes + 1) * LANES)
            for tile in range(count // TILE):
                field = [
                    [
                        mid_ref[pl.ds(kind * half + row * count + tile * TILE, TILE), across]
                        for kind in range(3)
                    ]
                    for row in range(COLORS)
                ]
                for pick in range(picks):
                    sums = [None] * 3
                    for row in range(COLORS):
                        at = COLORS * (COLORS * column + row)
                        for kind in range(3):
                            entry = jnp.broadcast_to(
                                matrices_ref[combo, at + kind, pick : pick + 1, across], (TILE, LANES)
                            )
                            term = entry * field[row][kind]
                            sums[kind] = term if row == 0 else sums[kind] + term
                    down = slice(pick * count + tile * TILE, pick * count + (tile + 1) * TILE)
                    at = 2 * column * sites + lanes * LANES
                    crossed_ref[down, at : at + LANES] = (sums[0] - sums[2]).astype(jnp.bfloat16)
                    at += sites
                    crossed_ref[down, at : at + LANES] = (sums[0] + sums[1]).astype(jnp.bfloat16)
        deep = slice(2 * column * sites, 2 * (column + 1) * sites)
        wide = slice(column * sites, (column + 1) * sites)
        part = lax.dot_general(
            crossed_ref[:, deep],
            jnp.concatenate([right_ref[combo, :, wide], turned_ref[combo, :, wide]], axis=1),
            (((1,), (1,)), ((), ())),
            preferred_element_type=jnp.float32,
        )
        result = part if result is None else result + part
    out_ref[combo] = result.reshape(out_ref.shape[1:]).astype(out_ref.dtype)


def moves_of(meta, layout):
    ring, combos = layout

    class Moves:
        def __getitem__(self, key):
            combo, slot = key
            return meta[ring + 3 * combo + slot]

    class Rows:
        shape = (meta.shape[0] - ring - 3 * combos,)

        def __getitem__(self, i):
            return meta[ring + 3 * combos + i]

    return Moves(), Rows()


def early_kernel(layout, scale, meta, here_ref, links_ref, shifts_ref, right_ref, matrices_ref, copy_ref, joins_ref):
    copy_ref[...] = here_ref[...]
    moves, rows = moves_of(meta, layout)
    for combo in range(layout[1]):
        join_links(combo, moves, links_ref, joins_ref, scale)
    for combo in range(layout[1]):

        @pl.when(moves[combo, 0] != 3)
        def _(combo=combo):
            shift = in_plane(shifts_ref, moves[combo, 0])
            site_matrices(combo, rows, here_ref, shift, joins_ref, matrices_ref)

        @pl.when(moves[combo, 2] != 3)
        def _(combo=combo):
            right_operand(combo, here_ref, in_plane(shifts_ref, moves[combo, 2]), right_ref)


def keep_right(combo, field, right_ref, turned_ref):
    vectors, sites = right_ref.shape[1] // 2, right_ref.shape[2] // COLORS
    for color in range(COLORS):
        wide = slice(color * sites, (color + 1) * sites)
        re, im = field(0, color), field(1, color)
        right_ref[combo, :vectors, wide] = re
        right_ref[combo, vectors:, wide] = im
        turned_ref[combo, :vectors, wide] = -im
        turned_ref[combo, vectors:, wide] = re


def first_kernel(layout, meta, here_ref, next_ref, joins_ref, shifts_ref, right_in, matrices_in, right_ref, matrices_ref, out_ref, turned_ref, mid_ref, crossed_ref):
    moves, rows = moves_of(meta, layout)
    vectors, sites = here_ref.shape[-2:]
    for combo in range(layout[1]):

        @pl.when(moves[combo, 0] == 3)
        def _(combo=combo):
            site_matrices(combo, rows, next_ref, None, joins_ref, matrices_ref)

        @pl.when(moves[combo, 0] != 3)
        def _(combo=combo):
            matrices_ref[combo] = matrices_in[combo]

        @pl.when(moves[combo, 2] == 3)
        def _(combo=combo):
            keep_right(combo, lambda part, color: next_ref[part, color], right_ref, turned_ref)

        @pl.when(moves[combo, 2] != 3)
        def _(combo=combo):
            def ready(part, color):
                return right_in[
                    combo, part * vectors : (part + 1) * vectors, color * sites : (color + 1) * sites
                ]

            keep_right(combo, ready, right_ref, turned_ref)

    for combo in range(layout[1]):
        row_block(combo, meta[0], moves, here_ref, next_ref, shifts_ref, matrices_ref, right_ref, turned_ref, mid_ref.at[combo], crossed_ref.at[combo], out_ref)


def block_kernel(number, layout, meta, here_ref, next_ref, shifts_ref, right_ref, matrices_ref, out_ref, turned_ref, mid_ref, crossed_ref):
    turn(right_ref, turned_ref)
    moves, _ = moves_of(meta, layout)
    for combo in range(layout[1]):
        row_block(combo, meta[number], moves, here_ref, next_ref, shifts_ref, matrices_ref, right_ref, turned_ref, mid_ref.at[combo], crossed_ref.at[combo], out_ref)


def local_work(eigenvectors, gauge_links, displacements, block_rows):
    parts, vectors, colors, planes, sites = eigenvectors.shape
    ring = lax.axis_size("site")
    me = lax.axis_index("site")
    combos, picks = displacements.shape[0], block_rows.shape[0]
    layout = (ring, combos)
    count = vectors // ring
    scale = 1.0 / math.sqrt(24.0 * planes * ring * sites)
    here = jnp.transpose(eigenvectors, (0, 2, 3, 1, 4)).reshape(parts, colors, vectors, sites)
    after = shifted(here, "site", -1)
    links = jnp.transpose(gauge_links, (1, 2, 3, 0, 4, 5)).astype(jnp.float32)
    links = links.reshape(COLORS, colors * colors * parts, sites)
    shifts = shift_matrices(sites, LX)
    last = ring - 1
    folded = ring == 4
    if folded:
        owners = [last - me, lax.rem(me + 2, ring), me + 1 - 2 * lax.rem(me, 2), me]
    else:
        owners = [lax.rem(me + offset, ring) for offset in range(1, ring + 1)]
    meta = jnp.concatenate(
        [jnp.stack(owners) * count, displacements.reshape(-1), block_rows]
    ).astype(jnp.int32)

    smem = pl.BlockSpec(memory_space=pltpu.SMEM)
    vmem = pl.BlockSpec(memory_space=pltpu.VMEM)
    right = jax.ShapeDtypeStruct((combos, parts * vectors, colors * sites), jnp.bfloat16)
    matrices = jax.ShapeDtypeStruct((combos, 3 * colors * colors, picks, sites), jnp.float32)
    joins = jax.ShapeDtypeStruct((combos, 2 * (1 + colors) * colors * colors, sites), jnp.float32)
    scratch = [
        pltpu.VMEM(right.shape, right.dtype),
        pltpu.VMEM((combos, 3 * colors * count, sites), jnp.float32),
        pltpu.VMEM((combos, picks * count, parts * colors * sites), jnp.bfloat16),
    ]
    params = pltpu.CompilerParams(vmem_limit_bytes=VMEM_BYTES)

    def chunk(kind):
        return jax.ShapeDtypeStruct((combos, picks, count, 2 * vectors), kind)

    right, matrices, here, joins = pl.pallas_call(
        functools.partial(early_kernel, layout, scale),
        out_shape=(right, matrices, jax.ShapeDtypeStruct(here.shape, here.dtype), joins),
        in_specs=[smem, vmem, vmem, vmem],
        out_specs=(vmem, vmem, vmem, vmem),
        compiler_params=params,
        cost_estimate=pl.CostEstimate(flops=500_000_000, bytes_accessed=4_000_000, transcendentals=0),
        name="early",
    )(meta, here, links, shifts)
    right, matrices, sent = pl.pallas_call(
        functools.partial(first_kernel, layout),
        out_shape=(
            jax.ShapeDtypeStruct(right.shape, right.dtype),
            jax.ShapeDtypeStruct(matrices.shape, matrices.dtype),
            chunk(jnp.bfloat16),
        ),
        in_specs=[smem, vmem, vmem, vmem, vmem, vmem, vmem],
        out_specs=(vmem, vmem, vmem),
        scratch_shapes=scratch,
        compiler_params=params,
        name="first",
    )(meta, here, after, joins, shifts, right, matrices)
    blocks = [sent]
    for number in range(1, ring):
        blocks.append(
            pl.pallas_call(
                functools.partial(block_kernel, number, layout),
                out_shape=chunk(jnp.float32 if number == last else jnp.bfloat16),
                in_specs=[smem, vmem, vmem, vmem, vmem, vmem],
                out_specs=vmem,
                scratch_shapes=scratch,
                compiler_params=params,
                cost_estimate=pl.CostEstimate(flops=1_000_000_000, bytes_accessed=4_000_000, transcendentals=0),
            )(meta, here, after, shifts, right, matrices)
        )
    own = blocks.pop()
    if not folded:
        arrived = [shifted(block, "site", offset + 1) for offset, block in enumerate(blocks)]
        return functools.reduce(lambda total, block: total + block.astype(jnp.float32), arrived, own)
    near = middle_exchange(blocks[0])
    near = jnp.where((me > 0) & (me < last), near, jnp.zeros_like(near))
    passed = lax.ppermute(blocks[0], "site", [(0, 1), (3, 2)])
    far = shifted(blocks[1] + passed, "site", 2)
    paired = lax.ppermute(blocks[2], "site", [(0, 1), (1, 0), (2, 3), (3, 2)])
    held = own + near.astype(jnp.float32) + paired.astype(jnp.float32)
    held = lax.optimization_barrier(held)
    return held + far.astype(jnp.float32)


def solution(mesh):
    step = jax.shard_map(
        local_work,
        mesh=mesh,
        in_specs=(
            P("ta", None, None, "site", None),
            P("ta", None, None, None, "site", None),
            P(),
            P(),
        ),
        out_specs=P("ta", None, "site", None),
        check_vma=False,
    )
    if mesh.shape["site"] != 4:
        return step
    return step
```

```python
import functools
import math

import jax
import jax.numpy as jnp
from jax import lax
from jax.experimental import pallas as pl
from jax.experimental.pallas import tpu as pltpu
from jax.sharding import PartitionSpec as P


LX = 16
COLORS = 3
TILE = 16
LANES = 128
SUBLANES = 8
VMEM_BYTES = 16 * 2**20


def shifted(block, axis, distance):
    count = lax.axis_size(axis)
    return lax.ppermute(block, axis, [(i, (i + distance) % count) for i in range(count)])


def shift_matrices(sites, width_x):
    source = lax.broadcasted_iota(jnp.int32, (COLORS, sites, sites), 1)
    target = lax.broadcasted_iota(jnp.int32, (COLORS, sites, sites), 2)
    direction = lax.broadcasted_iota(jnp.int32, (COLORS, sites, sites), 0)
    column = lax.rem(target, width_x)
    along_x = target - column + lax.rem(column + 1, width_x)
    along_y = lax.rem(target + width_x, sites)
    neighbour = jnp.where(direction == 1, along_x, jnp.where(direction == 2, along_y, target))
    return jnp.where(source == neighbour, 1.0, 0.0).astype(jnp.bfloat16)


def in_plane(shifts_ref, direction):
    return shifts_ref[jnp.where(direction == 3, 0, direction)]


def middle_exchange(block):
    lines, ring = lax.axis_size("ta"), lax.axis_size("site")
    route = []
    for line in range(lines):
        beside = line ^ 1 if lines % 2 == 0 else line
        for site in range(ring):
            inner = 0 < site < ring - 1
            target = line * ring + ring - 1 - site if inner else beside * ring + site
            route.append((line * ring + site, target))
    return lax.ppermute(block, ("ta", "site"), route)


def mul(left, right):
    return left[0] * right[0] - left[1] * right[1], left[0] * right[1] + left[1] * right[0]


def add(left, right):
    return left[0] + right[0], left[1] + right[1]


def chosen_link(links_ref, direction):
    which = jnp.maximum(direction - 1, 0)
    resting = direction == 0

    def entry(row, column):
        at = 2 * (COLORS * row + column)
        re = links_ref[which, at : at + 1, :]
        im = links_ref[which, at + 1 : at + 2, :]
        unit = jnp.full_like(re, 1.0 if row == column else 0.0)
        return jnp.where(resting, unit, re), jnp.where(resting, jnp.zeros_like(im), im)

    return [[entry(row, column) for column in range(COLORS)] for row in range(COLORS)]


def join_links(combo, moves, links_ref, joins_ref, scale):
    first, second, third = (chosen_link(links_ref, moves[combo, slot]) for slot in range(3))
    for a in range(COLORS):
        for b in range(COLORS):
            for part in range(2):
                at = 2 * (COLORS * a + b) + part
                joins_ref[combo, at : at + 1, :] = first[a][b][part] * scale
    for a in range(COLORS):
        up, down = (a + 1) % COLORS, (a + 2) % COLORS
        for column in range(COLORS):
            for row in range(COLORS):
                plus = mul(second[up][row], third[down][column])
                minus = mul(second[down][row], third[up][column])
                at = 2 * (COLORS * COLORS * (1 + a) + COLORS * column + row)
                for part in range(2):
                    joins_ref[combo, at + part : at + part + 1, :] = plus[part] - minus[part]


def site_matrices(combo, rows, plane_ref, shift, joins_ref, matrices_ref):
    vectors = plane_ref.shape[-2]
    kept, picks = matrices_ref.shape[2], SUBLANES
    numbers = lax.broadcasted_iota(jnp.int32, (picks, vectors), 1)
    lane = lax.broadcasted_iota(jnp.int32, (picks, vectors), 0)
    wanted = jnp.full((picks, vectors), -1, jnp.int32)
    for i in range(rows.shape[0]):
        wanted = jnp.where(lane == i, rows[i], wanted)
    select = jnp.where(numbers == wanted, 1.0, 0.0).astype(jnp.bfloat16)
    stacked = jnp.concatenate(
        [
            jnp.dot(select, plane_ref[part, color], preferred_element_type=jnp.float32)
            for color in range(COLORS)
            for part in range(2)
        ],
        axis=0,
    )
    if shift is not None:
        stacked = jnp.dot(stacked.astype(jnp.bfloat16), shift, preferred_element_type=jnp.float32)
    fields = [
        tuple(stacked[at * picks : (at + 1) * picks] for at in (2 * color, 2 * color + 1))
        for color in range(COLORS)
    ]

    def joined(at):
        return tuple(joins_ref[combo, 2 * at + part : 2 * at + part + 1, :] for part in range(2))

    def total(terms):
        return functools.reduce(add, terms)

    left = [
        total(mul(joined(COLORS * a + b), fields[b]) for b in range(COLORS)) for a in range(COLORS)
    ]
    for place in range(COLORS * COLORS):
        re, im = total(
            mul(joined(COLORS * COLORS * (1 + a) + place), left[a]) for a in range(COLORS)
        )
        at = COLORS * place
        matrices_ref[combo, at] = (re + im)[:kept]
        matrices_ref[combo, at + 1] = re[:kept]
        matrices_ref[combo, at + 2] = im[:kept]


def right_operand(combo, plane_ref, shift, right_ref):
    vectors, sites = plane_ref.shape[-2:]
    for color in range(COLORS):
        for part in range(2):
            field = jnp.dot(plane_ref[part, color], shift, preferred_element_type=jnp.float32)
            right_ref[
                combo, part * vectors : (part + 1) * vectors, color * sites : (color + 1) * sites
            ] = field.astype(right_ref.dtype)


def turn(right_ref, turned_ref):
    vectors = right_ref.shape[1] // 2
    for combo in range(right_ref.shape[0]):
        turned_ref[combo, :vectors] = -right_ref[combo, vectors:]
        turned_ref[combo, vectors:] = right_ref[combo, :vectors]


def row_block(combo, start, mids_ref, matrices_ref, right_ref, turned_ref, mid_ref, crossed_ref, out_ref):
    sites = mids_ref.shape[-1]
    picks, count = out_ref.shape[1:3]
    half = COLORS * count
    rows = pl.ds(pl.multiple_of(start, TILE), count)
    both = mids_ref[combo, :, :, rows].reshape(2 * half, sites).astype(jnp.float32)
    re, im = both[:half], both[half:]
    mid_ref[:half] = re
    mid_ref[half : 2 * half] = im - re
    mid_ref[2 * half :] = re + im
    result = None
    for column in range(COLORS):
        for lanes in range(sites // LANES):
            across = slice(lanes * LANES, (lanes + 1) * LANES)
            for tile in range(count // TILE):
                field = [
                    [
                        mid_ref[pl.ds(kind * half + row * count + tile * TILE, TILE), across]
                        for kind in range(3)
                    ]
                    for row in range(COLORS)
                ]
                for pick in range(picks):
                    sums = [None] * 3
                    for row in range(COLORS):
                        at = COLORS * (COLORS * column + row)
                        for kind in range(3):
                            entry = jnp.broadcast_to(
                                matrices_ref[combo, at + kind, pick : pick + 1, across], (TILE, LANES)
                            )
                            term = entry * field[row][kind]
                            sums[kind] = term if row == 0 else sums[kind] + term
                    down = slice(pick * count + tile * TILE, pick * count + (tile + 1) * TILE)
                    at = 2 * column * sites + lanes * LANES
                    crossed_ref[down, at : at + LANES] = (sums[0] - sums[2]).astype(jnp.bfloat16)
                    at += sites
                    crossed_ref[down, at : at + LANES] = (sums[0] + sums[1]).astype(jnp.bfloat16)
        deep = slice(2 * column * sites, 2 * (column + 1) * sites)
        wide = slice(column * sites, (column + 1) * sites)
        part = lax.dot_general(
            crossed_ref[:, deep],
            jnp.concatenate([right_ref[combo, :, wide], turned_ref[combo, :, wide]], axis=1),
            (((1,), (1,)), ((), ())),
            preferred_element_type=jnp.float32,
        )
        result = part if result is None else result + part
    out_ref[combo] = result.reshape(out_ref.shape[1:]).astype(out_ref.dtype)


def moves_of(meta, layout):
    ring, combos = layout

    class Moves:
        def __getitem__(self, key):
            combo, slot = key
            return meta[ring + 3 * combo + slot]

    class Rows:
        shape = (meta.shape[0] - ring - 3 * combos,)

        def __getitem__(self, i):
            return meta[ring + 3 * combos + i]

    return Moves(), Rows()


def early_kernel(layout, scale, meta, here_ref, links_ref, shifts_ref, right_ref, matrices_ref, mids_ref, joins_ref):
    moves, rows = moves_of(meta, layout)
    for combo in range(layout[1]):
        join_links(combo, moves, links_ref, joins_ref, scale)
    for combo in range(layout[1]):

        @pl.when(moves[combo, 0] != 3)
        def _(combo=combo):
            shift = in_plane(shifts_ref, moves[combo, 0])
            site_matrices(combo, rows, here_ref, shift, joins_ref, matrices_ref)

        @pl.when(moves[combo, 2] != 3)
        def _(combo=combo):
            right_operand(combo, here_ref, in_plane(shifts_ref, moves[combo, 2]), right_ref)

        @pl.when(moves[combo, 1] != 3)
        def _(combo=combo):
            shift = in_plane(shifts_ref, moves[combo, 1])
            for part in range(2):
                for color in range(COLORS):
                    field = jnp.dot(here_ref[part, color], shift, preferred_element_type=jnp.float32)
                    mids_ref[combo, part, color] = field.astype(mids_ref.dtype)


def keep_right(combo, field, right_ref, turned_ref):
    vectors, sites = right_ref.shape[1] // 2, right_ref.shape[2] // COLORS
    for color in range(COLORS):
        wide = slice(color * sites, (color + 1) * sites)
        re, im = field(0, color), field(1, color)
        right_ref[combo, :vectors, wide] = re
        right_ref[combo, vectors:, wide] = im
        turned_ref[combo, :vectors, wide] = -im
        turned_ref[combo, vectors:, wide] = re


def first_kernel(layout, meta, next_ref, joins_ref, right_in, matrices_in, mids_in, right_ref, matrices_ref, mids_ref, out_ref, turned_ref, mid_ref, crossed_ref):
    moves, rows = moves_of(meta, layout)
    vectors, sites = next_ref.shape[-2:]
    for combo in range(layout[1]):

        @pl.when(moves[combo, 1] == 3)
        def _(combo=combo):
            mids_ref[combo] = next_ref[...]

        @pl.when(moves[combo, 1] != 3)
        def _(combo=combo):
            mids_ref[combo] = mids_in[combo]

        @pl.when(moves[combo, 0] == 3)
        def _(combo=combo):
            site_matrices(combo, rows, next_ref, None, joins_ref, matrices_ref)

        @pl.when(moves[combo, 0] != 3)
        def _(combo=combo):
            matrices_ref[combo] = matrices_in[combo]

        @pl.when(moves[combo, 2] == 3)
        def _(combo=combo):
            keep_right(combo, lambda part, color: next_ref[part, color], right_ref, turned_ref)

        @pl.when(moves[combo, 2] != 3)
        def _(combo=combo):
            def ready(part, color):
                return right_in[
                    combo, part * vectors : (part + 1) * vectors, color * sites : (color + 1) * sites
                ]

            keep_right(combo, ready, right_ref, turned_ref)

    for combo in range(layout[1]):
        row_block(combo, meta[0], mids_ref, matrices_ref, right_ref, turned_ref, mid_ref.at[combo], crossed_ref.at[combo], out_ref)


def block_kernel(number, layout, meta, mids_ref, right_ref, matrices_ref, out_ref, turned_ref, mid_ref, crossed_ref):
    turn(right_ref, turned_ref)
    for combo in range(layout[1]):
        row_block(combo, meta[number], mids_ref, matrices_ref, right_ref, turned_ref, mid_ref.at[combo], crossed_ref.at[combo], out_ref)


def local_work(eigenvectors, gauge_links, displacements, block_rows):
    parts, vectors, colors, planes, sites = eigenvectors.shape
    ring = lax.axis_size("site")
    me = lax.axis_index("site")
    combos, picks = displacements.shape[0], block_rows.shape[0]
    layout = (ring, combos)
    count = vectors // ring
    scale = 1.0 / math.sqrt(24.0 * planes * ring * sites)
    here = jnp.transpose(eigenvectors, (0, 2, 3, 1, 4)).reshape(parts, colors, vectors, sites)
    after = shifted(here, "site", -1)
    links = jnp.transpose(gauge_links, (1, 2, 3, 0, 4, 5)).astype(jnp.float32)
    links = links.reshape(COLORS, colors * colors * parts, sites)
    shifts = shift_matrices(sites, LX)
    last = ring - 1
    folded = ring == 4
    if folded:
        owners = [last - me, lax.rem(me + 2, ring), me + 1 - 2 * lax.rem(me, 2), me]
    else:
        owners = [lax.rem(me + offset, ring) for offset in range(1, ring + 1)]
    meta = jnp.concatenate(
        [jnp.stack(owners) * count, displacements.reshape(-1), block_rows]
    ).astype(jnp.int32)

    smem = pl.BlockSpec(memory_space=pltpu.SMEM)
    vmem = pl.BlockSpec(memory_space=pltpu.VMEM)
    right = jax.ShapeDtypeStruct((combos, parts * vectors, colors * sites), jnp.bfloat16)
    matrices = jax.ShapeDtypeStruct((combos, 3 * colors * colors, picks, sites), jnp.float32)
    joins = jax.ShapeDtypeStruct((combos, 2 * (1 + colors) * colors * colors, sites), jnp.float32)
    scratch = [
        pltpu.VMEM(right.shape, right.dtype),
        pltpu.VMEM((combos, 3 * colors * count, sites), jnp.float32),
        pltpu.VMEM((combos, picks * count, parts * colors * sites), jnp.bfloat16),
    ]
    params = pltpu.CompilerParams(vmem_limit_bytes=VMEM_BYTES)

    def chunk(kind):
        return jax.ShapeDtypeStruct((combos, picks, count, 2 * vectors), kind)

    right, matrices, mids, joins = pl.pallas_call(
        functools.partial(early_kernel, layout, scale),
        out_shape=(right, matrices, jax.ShapeDtypeStruct((combos, *here.shape), here.dtype), joins),
        in_specs=[smem, vmem, vmem, vmem],
        out_specs=(vmem, vmem, vmem, vmem),
        compiler_params=params,
        cost_estimate=pl.CostEstimate(flops=500_000_000, bytes_accessed=4_000_000, transcendentals=0),
        name="early",
    )(meta, here, links, shifts)
    right, matrices, mids, sent = pl.pallas_call(
        functools.partial(first_kernel, layout),
        out_shape=(
            jax.ShapeDtypeStruct(right.shape, right.dtype),
            jax.ShapeDtypeStruct(matrices.shape, matrices.dtype),
            jax.ShapeDtypeStruct(mids.shape, mids.dtype),
            chunk(jnp.bfloat16),
        ),
        in_specs=[smem, vmem, vmem, vmem, vmem, vmem],
        out_specs=(vmem, vmem, vmem, vmem),
        input_output_aliases={3: 0, 4: 1, 5: 2},
        scratch_shapes=scratch,
        compiler_params=params,
        name="first",
    )(meta, after, joins, right, matrices, mids)
    blocks = [sent]
    for number in range(1, ring):
        blocks.append(
            pl.pallas_call(
                functools.partial(block_kernel, number, layout),
                out_shape=chunk(jnp.float32 if number == last else jnp.bfloat16),
                in_specs=[smem, vmem, vmem, vmem],
                out_specs=vmem,
                scratch_shapes=scratch,
                compiler_params=params,
                cost_estimate=pl.CostEstimate(flops=1_000_000_000, bytes_accessed=4_000_000, transcendentals=0),
            )(meta, mids, right, matrices)
        )
    own = blocks.pop()
    if not folded:
        arrived = [shifted(block, "site", offset + 1) for offset, block in enumerate(blocks)]
        return functools.reduce(lambda total, block: total + block.astype(jnp.float32), arrived, own)
    near = middle_exchange(blocks[0])
    near = jnp.where((me > 0) & (me < last), near, jnp.zeros_like(near))
    passed = lax.ppermute(blocks[0], "site", [(0, 1), (3, 2)])
    far = shifted(blocks[1] + passed, "site", 2)
    paired = lax.ppermute(blocks[2], "site", [(0, 1), (1, 0), (2, 3), (3, 2)])
    held = own + near.astype(jnp.float32) + paired.astype(jnp.float32)
    held = lax.optimization_barrier(held)
    return held + far.astype(jnp.float32)


def solution(mesh):
    step = jax.shard_map(
        local_work,
        mesh=mesh,
        in_specs=(
            P("ta", None, None, "site", None),
            P("ta", None, None, None, "site", None),
            P(),
            P(),
        ),
        out_specs=P("ta", None, "site", None),
        check_vma=False,
    )
    if mesh.shape["site"] != 4:
        return step
    return step
```

```python
import functools
import math

import jax
import jax.numpy as jnp
from jax import lax
from jax.experimental import pallas as pl
from jax.experimental.pallas import tpu as pltpu
from jax.sharding import PartitionSpec as P


LX = 16
COLORS = 3
TILE = 16
LANES = 128
SUBLANES = 8
VMEM_BYTES = 16 * 2**20


def shifted(block, axis, distance):
    count = lax.axis_size(axis)
    return lax.ppermute(block, axis, [(i, (i + distance) % count) for i in range(count)])


def shift_matrices(sites, width_x):
    source = lax.broadcasted_iota(jnp.int32, (COLORS, sites, sites), 1)
    target = lax.broadcasted_iota(jnp.int32, (COLORS, sites, sites), 2)
    direction = lax.broadcasted_iota(jnp.int32, (COLORS, sites, sites), 0)
    column = lax.rem(target, width_x)
    along_x = target - column + lax.rem(column + 1, width_x)
    along_y = lax.rem(target + width_x, sites)
    neighbour = jnp.where(direction == 1, along_x, jnp.where(direction == 2, along_y, target))
    return jnp.where(source == neighbour, 1.0, 0.0).astype(jnp.bfloat16)


def in_plane(shifts_ref, direction):
    return shifts_ref[jnp.where(direction == 3, 0, direction)]


def mul(left, right):
    return left[0] * right[0] - left[1] * right[1], left[0] * right[1] + left[1] * right[0]


def add(left, right):
    return left[0] + right[0], left[1] + right[1]


def chosen_link(links_ref, direction):
    which = jnp.maximum(direction - 1, 0)
    resting = direction == 0

    def entry(row, column):
        at = 2 * (COLORS * row + column)
        re = links_ref[which, at : at + 1, :]
        im = links_ref[which, at + 1 : at + 2, :]
        unit = jnp.full_like(re, 1.0 if row == column else 0.0)
        return jnp.where(resting, unit, re), jnp.where(resting, jnp.zeros_like(im), im)

    return [[entry(row, column) for column in range(COLORS)] for row in range(COLORS)]


def join_links(combo, moves, links_ref, joins_ref, scale):
    first, second, third = (chosen_link(links_ref, moves[combo, slot]) for slot in range(3))
    for a in range(COLORS):
        for b in range(COLORS):
            for part in range(2):
                at = 2 * (COLORS * a + b) + part
                joins_ref[combo, at : at + 1, :] = first[a][b][part] * scale
    for a in range(COLORS):
        up, down = (a + 1) % COLORS, (a + 2) % COLORS
        for column in range(COLORS):
            for row in range(COLORS):
                plus = mul(second[up][row], third[down][column])
                minus = mul(second[down][row], third[up][column])
                at = 2 * (COLORS * COLORS * (1 + a) + COLORS * column + row)
                for part in range(2):
                    joins_ref[combo, at + part : at + part + 1, :] = plus[part] - minus[part]


def site_matrices(combo, rows, plane_ref, shift, joins_ref, matrices_ref):
    vectors = plane_ref.shape[-2]
    kept, picks = matrices_ref.shape[2], SUBLANES
    numbers = lax.broadcasted_iota(jnp.int32, (picks, vectors), 1)
    lane = lax.broadcasted_iota(jnp.int32, (picks, vectors), 0)
    wanted = jnp.full((picks, vectors), -1, jnp.int32)
    for i in range(rows.shape[0]):
        wanted = jnp.where(lane == i, rows[i], wanted)
    select = jnp.where(numbers == wanted, 1.0, 0.0).astype(jnp.bfloat16)
    stacked = jnp.concatenate(
        [
            jnp.dot(select, plane_ref[part, color], preferred_element_type=jnp.float32)
            for color in range(COLORS)
            for part in range(2)
        ],
        axis=0,
    )
    if shift is not None:
        stacked = jnp.dot(stacked.astype(jnp.bfloat16), shift, preferred_element_type=jnp.float32)
    fields = [
        tuple(stacked[at * picks : (at + 1) * picks] for at in (2 * color, 2 * color + 1))
        for color in range(COLORS)
    ]

    def joined(at):
        return tuple(joins_ref[combo, 2 * at + part : 2 * at + part + 1, :] for part in range(2))

    def total(terms):
        return functools.reduce(add, terms)

    left = [
        total(mul(joined(COLORS * a + b), fields[b]) for b in range(COLORS)) for a in range(COLORS)
    ]
    for place in range(COLORS * COLORS):
        re, im = total(
            mul(joined(COLORS * COLORS * (1 + a) + place), left[a]) for a in range(COLORS)
        )
        at = COLORS * place
        matrices_ref[combo, at] = (re + im)[:kept]
        matrices_ref[combo, at + 1] = re[:kept]
        matrices_ref[combo, at + 2] = im[:kept]


def right_operand(combo, plane_ref, shift, right_ref):
    vectors, sites = plane_ref.shape[-2:]
    for color in range(COLORS):
        for part in range(2):
            field = jnp.dot(plane_ref[part, color], shift, preferred_element_type=jnp.float32)
            right_ref[
                combo, part * vectors : (part + 1) * vectors, color * sites : (color + 1) * sites
            ] = field.astype(right_ref.dtype)


def turn(right_ref, turned_ref):
    vectors = right_ref.shape[1] // 2
    for combo in range(right_ref.shape[0]):
        turned_ref[combo, :vectors] = -right_ref[combo, vectors:]
        turned_ref[combo, vectors:] = right_ref[combo, :vectors]


def row_block(combo, start, mids_ref, matrices_ref, right_ref, turned_ref, mid_ref, crossed_ref, out_ref):
    sites = mids_ref.shape[-1]
    picks, count = out_ref.shape[1:3]
    half = COLORS * count
    rows = pl.ds(pl.multiple_of(start, TILE), count)
    both = mids_ref[combo, :, :, rows].reshape(2 * half, sites).astype(jnp.float32)
    re, im = both[:half], both[half:]
    mid_ref[:half] = re
    mid_ref[half : 2 * half] = im - re
    mid_ref[2 * half :] = re + im
    result = None
    for column in range(COLORS):
        for lanes in range(sites // LANES):
            across = slice(lanes * LANES, (lanes + 1) * LANES)
            for tile in range(count // TILE):
                field = [
                    [
                        mid_ref[pl.ds(kind * half + row * count + tile * TILE, TILE), across]
                        for kind in range(3)
                    ]
                    for row in range(COLORS)
                ]
                for pick in range(picks):
                    sums = [None] * 3
                    for row in range(COLORS):
                        at = COLORS * (COLORS * column + row)
                        for kind in range(3):
                            entry = jnp.broadcast_to(
                                matrices_ref[combo, at + kind, pick : pick + 1, across], (TILE, LANES)
                            )
                            term = entry * field[row][kind]
                            sums[kind] = term if row == 0 else sums[kind] + term
                    down = slice(pick * count + tile * TILE, pick * count + (tile + 1) * TILE)
                    at = 2 * column * sites + lanes * LANES
                    crossed_ref[down, at : at + LANES] = (sums[0] - sums[2]).astype(jnp.bfloat16)
                    at += sites
                    crossed_ref[down, at : at + LANES] = (sums[0] + sums[1]).astype(jnp.bfloat16)
        deep = slice(2 * column * sites, 2 * (column + 1) * sites)
        wide = slice(column * sites, (column + 1) * sites)
        part = lax.dot_general(
            crossed_ref[:, deep],
            jnp.concatenate([right_ref[combo, :, wide], turned_ref[combo, :, wide]], axis=1),
            (((1,), (1,)), ((), ())),
            preferred_element_type=jnp.float32,
        )
        result = part if result is None else result + part
    out_ref[combo] = result.reshape(out_ref.shape[1:]).astype(out_ref.dtype)


def moves_of(meta, layout):
    ring, combos = layout

    class Moves:
        def __getitem__(self, key):
            combo, slot = key
            return meta[ring + 3 * combo + slot]

    class Rows:
        shape = (meta.shape[0] - ring - 3 * combos,)

        def __getitem__(self, i):
            return meta[ring + 3 * combos + i]

    return Moves(), Rows()


def early_kernel(layout, scale, meta, here_ref, links_ref, shifts_ref, right_ref, matrices_ref, mids_ref, joins_ref):
    moves, rows = moves_of(meta, layout)
    for combo in range(layout[1]):
        join_links(combo, moves, links_ref, joins_ref, scale)
    for combo in range(layout[1]):

        @pl.when(moves[combo, 0] != 3)
        def _(combo=combo):
            shift = in_plane(shifts_ref, moves[combo, 0])
            site_matrices(combo, rows, here_ref, shift, joins_ref, matrices_ref)

        @pl.when(moves[combo, 2] != 3)
        def _(combo=combo):
            right_operand(combo, here_ref, in_plane(shifts_ref, moves[combo, 2]), right_ref)

        @pl.when(moves[combo, 1] != 3)
        def _(combo=combo):
            shift = in_plane(shifts_ref, moves[combo, 1])
            for part in range(2):
                for color in range(COLORS):
                    field = jnp.dot(here_ref[part, color], shift, preferred_element_type=jnp.float32)
                    mids_ref[combo, part, color] = field.astype(mids_ref.dtype)


def keep_right(combo, field, right_ref, turned_ref):
    vectors, sites = right_ref.shape[1] // 2, right_ref.shape[2] // COLORS
    for color in range(COLORS):
        wide = slice(color * sites, (color + 1) * sites)
        re, im = field(0, color), field(1, color)
        right_ref[combo, :vectors, wide] = re
        right_ref[combo, vectors:, wide] = im
        turned_ref[combo, :vectors, wide] = -im
        turned_ref[combo, vectors:, wide] = re


def first_kernel(layout, meta, next_ref, joins_ref, right_in, matrices_in, mids_in, right_ref, matrices_ref, mids_ref, out_ref, turned_ref, mid_ref, crossed_ref):
    moves, rows = moves_of(meta, layout)
    vectors, sites = next_ref.shape[-2:]
    for combo in range(layout[1]):

        @pl.when(moves[combo, 1] == 3)
        def _(combo=combo):
            mids_ref[combo] = next_ref[...]

        @pl.when(moves[combo, 1] != 3)
        def _(combo=combo):
            mids_ref[combo] = mids_in[combo]

        @pl.when(moves[combo, 0] == 3)
        def _(combo=combo):
            site_matrices(combo, rows, next_ref, None, joins_ref, matrices_ref)

        @pl.when(moves[combo, 0] != 3)
        def _(combo=combo):
            matrices_ref[combo] = matrices_in[combo]

        @pl.when(moves[combo, 2] == 3)
        def _(combo=combo):
            keep_right(combo, lambda part, color: next_ref[part, color], right_ref, turned_ref)

        @pl.when(moves[combo, 2] != 3)
        def _(combo=combo):
            def ready(part, color):
                return right_in[
                    combo, part * vectors : (part + 1) * vectors, color * sites : (color + 1) * sites
                ]

            keep_right(combo, ready, right_ref, turned_ref)

    for combo in range(layout[1]):
        row_block(combo, meta[0], mids_ref, matrices_ref, right_ref, turned_ref, mid_ref.at[combo], crossed_ref.at[combo], out_ref)


def block_kernel(number, layout, meta, mids_ref, right_ref, matrices_ref, out_ref, turned_ref, mid_ref, crossed_ref):
    turn(right_ref, turned_ref)
    for combo in range(layout[1]):
        row_block(combo, meta[number], mids_ref, matrices_ref, right_ref, turned_ref, mid_ref.at[combo], crossed_ref.at[combo], out_ref)


def local_work(eigenvectors, gauge_links, displacements, block_rows):
    parts, vectors, colors, planes, sites = eigenvectors.shape
    ring = lax.axis_size("site")
    me = lax.axis_index("site")
    combos, picks = displacements.shape[0], block_rows.shape[0]
    layout = (ring, combos)
    count = vectors // ring
    scale = 1.0 / math.sqrt(24.0 * planes * ring * sites)
    here = jnp.transpose(eigenvectors, (0, 2, 3, 1, 4)).reshape(parts, colors, vectors, sites)
    after = shifted(here, "site", -1)
    links = jnp.transpose(gauge_links, (1, 2, 3, 0, 4, 5)).astype(jnp.float32)
    links = links.reshape(COLORS, colors * colors * parts, sites)
    shifts = shift_matrices(sites, LX)
    last = ring - 1
    folded = ring == 4
    if folded:
        owners = [last - me, lax.rem(me + 2, ring), me + 1 - 2 * lax.rem(me, 2), me]
    else:
        owners = [lax.rem(me + offset, ring) for offset in range(1, ring + 1)]
    meta = jnp.concatenate(
        [jnp.stack(owners) * count, displacements.reshape(-1), block_rows]
    ).astype(jnp.int32)

    smem = pl.BlockSpec(memory_space=pltpu.SMEM)
    vmem = pl.BlockSpec(memory_space=pltpu.VMEM)
    right = jax.ShapeDtypeStruct((combos, parts * vectors, colors * sites), jnp.bfloat16)
    matrices = jax.ShapeDtypeStruct((combos, 3 * colors * colors, picks, sites), jnp.float32)
    joins = jax.ShapeDtypeStruct((combos, 2 * (1 + colors) * colors * colors, sites), jnp.float32)
    scratch = [
        pltpu.VMEM(right.shape, right.dtype),
        pltpu.VMEM((combos, 3 * colors * count, sites), jnp.float32),
        pltpu.VMEM((combos, picks * count, parts * colors * sites), jnp.bfloat16),
    ]
    params = pltpu.CompilerParams(vmem_limit_bytes=VMEM_BYTES)

    def chunk(kind):
        return jax.ShapeDtypeStruct((combos, picks, count, 2 * vectors), kind)

    right, matrices, mids, joins = pl.pallas_call(
        functools.partial(early_kernel, layout, scale),
        out_shape=(right, matrices, jax.ShapeDtypeStruct((combos, *here.shape), here.dtype), joins),
        in_specs=[smem, vmem, vmem, vmem],
        out_specs=(vmem, vmem, vmem, vmem),
        compiler_params=params,
        cost_estimate=pl.CostEstimate(flops=500_000_000, bytes_accessed=4_000_000, transcendentals=0),
        name="early",
    )(meta, here, links, shifts)
    right, matrices, mids, sent = pl.pallas_call(
        functools.partial(first_kernel, layout),
        out_shape=(
            jax.ShapeDtypeStruct(right.shape, right.dtype),
            jax.ShapeDtypeStruct(matrices.shape, matrices.dtype),
            jax.ShapeDtypeStruct(mids.shape, mids.dtype),
            chunk(jnp.bfloat16),
        ),
        in_specs=[smem, vmem, vmem, vmem, vmem, vmem],
        out_specs=(vmem, vmem, vmem, vmem),
        input_output_aliases={3: 0, 4: 1, 5: 2},
        scratch_shapes=scratch,
        compiler_params=params,
        name="first",
    )(meta, after, joins, right, matrices, mids)
    blocks = [sent]
    for number in range(1, ring):
        blocks.append(
            pl.pallas_call(
                functools.partial(block_kernel, number, layout),
                out_shape=chunk(jnp.float32 if number == last else jnp.bfloat16),
                in_specs=[smem, vmem, vmem, vmem],
                out_specs=vmem,
                scratch_shapes=scratch,
                compiler_params=params,
                cost_estimate=pl.CostEstimate(flops=1_000_000_000, bytes_accessed=4_000_000, transcendentals=0),
            )(meta, mids, right, matrices)
        )
    own = blocks.pop()
    if not folded:
        arrived = [shifted(block, "site", offset + 1) for offset, block in enumerate(blocks)]
        return functools.reduce(lambda total, block: total + block.astype(jnp.float32), arrived, own)
    near = lax.ppermute(blocks[0], "site", [(1, 2), (2, 1)])
    passed = lax.ppermute(blocks[0], "site", [(0, 1), (3, 2)])
    far = shifted(blocks[1] + passed, "site", 2)
    paired = lax.ppermute(blocks[2], "site", [(0, 1), (1, 0), (2, 3), (3, 2)])
    held = own + near.astype(jnp.float32) + paired.astype(jnp.float32)
    held = lax.optimization_barrier(held)
    return held + far.astype(jnp.float32)


def solution(mesh):
    step = jax.shard_map(
        local_work,
        mesh=mesh,
        in_specs=(
            P("ta", None, None, "site", None),
            P("ta", None, None, None, "site", None),
            P(),
            P(),
        ),
        out_specs=P("ta", None, "site", None),
        check_vma=False,
    )
    if mesh.shape["site"] != 4:
        return step
    return step
```
